128 devices in a mesh: row: 16 (over y, x), col: 8 (over z, core).
Axes of the slice: x: 4, y: 4, z: 4, core: 2. Of those that a mesh axis runs over, the one named last changes fastest.
Arguments:
- white_noise: float32 [8192, 8192], P('row', 'col'), may hold values from -6 to 6
- amplitude: float32 [8192, 8192], P(('row', 'col')), may hold values from 0.3 to 3
- state_prev: float32 [8192, 8192], P('row', 'col'), may hold values from -6 to 6
- catch_id: int32 [64, 64], P('row', 'col'), may hold values from 0 to 2047
- owner_map: int32 [2048, 1], replicated, may hold values from 0 to 127; in each aligned block of 2048 rows (0 to 2047, 2048 to 4095, ...) at most 32 rows name the same one
- unit_graph: float32 [288, 4096], P(None, ('row', 'col')), may hold values from 0.05 to 0.5
- queue_prev: float32 [288, 4096], P(None, ('row', 'col')), may hold values from -6 to 6
Outputs:
- state_new: float32 [8192, 8192], P('row', 'col')
- flow_queue: float32 [288, 4096], P(None, ('row', 'col'))
The draws below stay inside these ranges and needn't reach their ends.
Inputs may be any that keep to these rules, and one draw needn't show every extreme that they name: `owner_map`: each device owns at most 32 catchments, and some device owns exactly 32.
All inputs are finite; a program needn't handle non-finite values.
Results may differ from the reference program's by a relative error of at most 0.000088.
Values sent between devices are 32-bit elements; how exact they have to be, the bound alone decides.
No kernel may reach another device: no remote copies, remote signals or barrier semaphores. Data moves between devices by JAX's collectives and lax.ppermute only.
A program may use at most 128 MiB of HBM per device.

```python
import math
import jax
import jax.numpy as jnp
import numpy as np

GRID = 8192
TILE = 128
LAGS = 288
CAP = 32
CATCH = 2048
SLOTS = 4096
TILES = 64
N_ROW = 16
N_COL = 8


def plant(values, rng, smallest, top_value):
    longest = values.shape.index(max(values.shape))
    spots = []
    for shift in (0, 1):
        where = [jax.random.randint(jax.random.fold_in(rng, axis), (), 0, length) for axis, length in enumerate(values.shape)]
        where[longest] = (where[longest] + shift) % values.shape[longest]
        spots.append(tuple(where))
    return values.at[spots[0]].set(smallest).at[spots[1]].set(top_value)


def level_of(stream_key, extent, cuts, low, largest):
    def one(position, shards_of):
        draws = jax.random.uniform(jax.random.fold_in(jax.random.fold_in(stream_key, 6), position), (shards_of,), jnp.float32, low / len(cuts), largest / len(cuts))
        return jnp.repeat(jnp.exp(draws), extent[position] // shards_of).reshape((-1,) + (1,) * (len(extent) - position - 1))

    level = one(*cuts[0])
    for cut in cuts[1:]:
        level = level * one(*cut)
    return level


def deal_out(own_key, own, number, rows, number_of, top, limit, lean):
    sequence = jax.random.permutation(own_key, number_of)
    heavy_load, usual = portions_of(number_of, rows * top, limit, lean, True), portions_of(number_of, rows * top, limit, lean, False)
    places = jnp.arange(number_of)

    def named(tallies, rotation):
        used = int((tallies > 0).sum())
        fixed = max(1, used // 4)
        moved = fixed + (places - fixed + rotation * (used - fixed)) % max(1, number_of - fixed)
        return jnp.zeros((number_of,), jnp.int32).at[sequence[jnp.where(places < fixed, places, moved)]].set(jnp.asarray(tallies, jnp.int32))

    tallies = jnp.where(number % 4 == 0, named(heavy_load, number // 4), named(usual, number - number // 4 - 1))
    mixed = jax.random.permutation(jax.random.fold_in(own, 3), number_of)
    source_of, receiver = mixed[0:number_of // 2 * 2:2], mixed[1:number_of // 2 * 2:2]
    margin = jnp.minimum(tallies[source_of] - 1, limit - tallies[receiver]) // 2
    margin = jnp.where((source_of == sequence[0]) | (receiver == sequence[0]) | (tallies[receiver] == 0), 0, jnp.maximum(margin, 0))
    moved = jax.random.randint(jax.random.fold_in(own, 4), (number_of // 2,), 0, 1 << 20) % (margin + 1)
    tallies = tallies.at[source_of].add(-moved).at[receiver].add(moved)
    members = jnp.searchsorted(jnp.cumsum(tallies), jnp.arange(rows * top), side="right").astype(jnp.int32)
    grid = members.reshape(top, rows).T
    grid = grid[jax.random.permutation(jax.random.fold_in(own, 1), rows)]
    rotation = jax.random.randint(jax.random.fold_in(own, 2), (rows, 1), 0, top)
    return jnp.take_along_axis(grid, (jnp.arange(top)[None, :] + rotation) % top, axis=1)


def portions_of(count, total, most, lean, full):
    portions = [(1 << 20) // math.isqrt(standing ** lean) + 1 for standing in range(1, count + 1)]
    largest = most if full else min(most, max(-(-total // count), total * portions[0] // sum(portions)))
    least = 1 if total - largest >= count - 1 else 0
    counts, spare = [largest] + [least] * (count - 1), total - largest - least * (count - 1)
    while spare > 0:
        candidates = [i for i in range(1, count) if counts[i] < largest] or [i for i in range(1, count) if counts[i] < most]
        pool, left = sum([portions[i] for i in candidates]), spare
        for i in candidates:
            extra = min(most - counts[i], max(1, left * portions[i] // pool), spare)
            counts[i] = counts[i] + extra
            spare = spare - extra
    return np.array(counts)


def centred(own_key, dims, scale, limit, shards=(), kind=jnp.bfloat16):
    drawn = jax.random.normal(own_key, dims, jnp.float32) * scale
    if len(shards) > 0:
        drawn = level_of(own_key, dims, shards, -0.22, 0.18) * drawn
    return jnp.clip(drawn, min=-limit, max=limit).astype(kind)


def setup_inputs(seed: int = 0) -> dict:
    key_list = jax.random.split(jax.random.key(seed), 8)
    white_noise = centred(key_list[0], (GRID, GRID), 1.0, 6.0, ((0, 16), (1, 8)), jnp.float32)
    amplitude = jnp.clip(jnp.exp(math.log(3.0) - 2.3025851 * jax.random.uniform(key_list[1], (GRID, GRID), jnp.float32) ** level_of(key_list[1], (GRID, GRID), ((0, 128),), -0.2, 0.2)), 0.3, 3.0)
    state_prev = centred(key_list[2], (GRID, GRID), 1.0, 6.0, ((0, 16), (1, 8)), jnp.float32)
    catch_id = plant(jax.random.randint(key_list[3], (TILES, TILES), 0, CATCH), jax.random.fold_in(key_list[3], 1), 0, CATCH - 1).astype(jnp.int32)
    owner_map_keys = jax.random.split(jax.random.fold_in(key_list[4], 1), CATCH // CATCH)
    owner_map_turns = jax.random.permutation(jax.random.fold_in(key_list[4], 3), CATCH // CATCH)
    owner_map = jax.vmap(lambda own, number: deal_out(jax.random.fold_in(key_list[4], 2), own, number, CATCH, N_ROW * N_COL, 1, CAP, 2))(owner_map_keys, owner_map_turns).reshape((CATCH, 1))
    unit_graph = jnp.clip(jnp.exp(math.log(0.5) - 2.3025851 * jax.random.uniform(key_list[5], (LAGS, SLOTS), jnp.float32) ** level_of(key_list[5], (LAGS, SLOTS), ((1, 128),), -0.2, 0.2)), 0.05, 0.5)
    queue_prev = centred(key_list[6], (LAGS, SLOTS), 1.0, 6.0, ((1, 128),), jnp.float32)
    return {"white_noise": white_noise, "amplitude": amplitude, "state_prev": state_prev, "catch_id": catch_id, "owner_map": owner_map, "unit_graph": unit_graph, "queue_prev": queue_prev}


bump_height = 64.0
persist = 0.8
innovate = 0.6
log_mean = -0.3
log_scale = 0.6


def signed_wave(length):
    counter = jnp.arange(length, dtype=jnp.int32)
    return jnp.where(counter < length // 2, counter, counter - length).astype(jnp.float32)


def reference(white_noise, amplitude, state_prev, catch_id, owner_map, unit_graph, queue_prev):
    waves = signed_wave(GRID)
    width_sq = float((GRID // 128) * (GRID // 128))
    envelope = 1.0 + bump_height / (1.0 + (waves[:, None] * waves[:, None] + waves[None, :] * waves[None, :]) / width_sq)
    spectrum = jnp.fft.fft2(white_noise)
    shaped = spectrum * (amplitude.T * envelope)
    filtered = jnp.real(jnp.fft.ifft2(shaped)).astype(jnp.float32)
    state_new = persist * state_prev + innovate * filtered
    rain = jnp.exp(log_mean + log_scale * state_new)
    tile_rain = rain.reshape(TILES, TILE, TILES, TILE).mean(axis=(1, 3))
    owners = owner_map[:, 0]
    hits = (owners[:, None] == jnp.arange(N_ROW * N_COL, dtype=jnp.int32)[None, :]).astype(jnp.int32)
    ranks = jnp.sum(hits * (jnp.cumsum(hits, axis=0) - 1), axis=1)
    slot = (owners * CAP + ranks).astype(jnp.int32)
    tile_slot = slot[catch_id].reshape(-1)
    slot_rain = jax.ops.segment_sum(tile_rain.reshape(-1), tile_slot, num_segments=SLOTS)
    shifted = jnp.concatenate([queue_prev[1:], jnp.zeros((1, SLOTS), queue_prev.dtype)], axis=0)
    flow_queue = shifted + unit_graph * slot_rain[None, :]
    return state_new, flow_queue
```

```python
from functools import partial

import jax
import jax.numpy as jnp
import ml_dtypes
import numpy as np
from jax import lax
from jax.experimental import pallas as pl
from jax.experimental.pallas import tpu as pltpu
from jax.sharding import PartitionSpec as P

TILE = 128
CAP = 32
N = 8192
DEV = 128
HALF = 32
BOTH = ("row", "col")

bump_height = 64.0
persist = 0.8
innovate = 0.6
log_mean = -0.3
log_scale = 0.6

BF = jnp.bfloat16
F32 = jnp.float32


def hi_lo(table):
    table = np.asarray(table, np.float64)
    hi = table.astype(ml_dtypes.bfloat16)
    lo = (table - hi.astype(np.float64)).astype(ml_dtypes.bfloat16)
    return np.concatenate([hi, lo], axis=1)


def angle(left, right, length):
    return 2.0 * np.pi / length * (np.outer(left, right) % length)


def real_forward():
    turn = angle(np.arange(64), np.arange(64), 64)
    table = np.concatenate([np.cos(turn[:33]), -np.sin(turn[1:32])], axis=0)
    return hi_lo(np.kron(table, np.eye(8)))


def real_inverse():
    turn = angle(np.arange(64), np.arange(64), 64)
    real = 2.0 * np.cos(turn[:, :33])
    real[:, 0] = 1.0
    table = np.concatenate([real, -2.0 * np.sin(turn[:, 1:32])], axis=1)
    return hi_lo(np.kron(table, np.eye(8)))


def row_twiddle():
    turn = angle(np.arange(33), np.arange(128), N)
    return np.concatenate([np.cos(turn), np.sin(turn)], axis=1).astype(np.float32)


def row_forward():
    turn = angle(np.arange(128), np.arange(128), 128)
    cos, sin = np.cos(turn), np.sin(turn)
    whole = np.block([[cos, sin], [-sin, cos]])
    low = (np.arange(128) < 64).astype(np.float64)[:, None]
    first = np.block([[cos * low, sin * low], [-sin * low, cos * low]])
    imag = -sin * (1 - low)
    imag[64] = 1.0
    last = np.concatenate([cos * (1 - low), imag], axis=0)
    return hi_lo(whole), hi_lo(np.concatenate([whole, first, last], axis=1))


def row_inverse():
    turn = angle(np.arange(128), np.arange(128), 128)
    cos, sin = np.cos(turn), np.sin(turn)
    whole = np.block([[cos, sin], [-sin, cos]])
    low = (np.arange(128) < 64).astype(np.float64)[:, None]
    first = np.block([[cos * low, sin * low], [-sin * low, cos * low]])
    top, bottom = 2.0 * cos * (1 - low), -2.0 * sin * (1 - low)
    top[64] = cos[64]
    bottom[64] = 1.0
    last = np.concatenate([top, bottom], axis=0)
    both = np.concatenate([first, last], axis=1)
    return hi_lo(whole), hi_lo(both)


def col_tables(sign):
    turn = angle(np.arange(128), np.arange(128), 128)
    cos, sin = np.cos(turn), sign * np.sin(turn)
    long = np.block([[cos, -sin], [sin, cos]])
    turn = angle(np.arange(64), np.arange(64), 64)
    cos, sin = np.kron(np.eye(2), np.cos(turn)), np.kron(np.eye(2), sign * np.sin(turn))
    short = np.block([[cos, sin], [-sin, cos]])
    return hi_lo(long), hi_lo(short)


def col_twiddle():
    turn = angle(np.arange(128), np.arange(128) % 64, N)
    return np.concatenate([np.cos(turn), np.sin(turn)], axis=1).astype(np.float32)


def split(value):
    hi = value.astype(BF)
    return hi, (value - hi.astype(F32)).astype(BF)


def dot(left, right, dims=((1,), (0,))):
    return lax.dot_general(left, right, (dims, ((), ())), preferred_element_type=F32)


def times_table(value, table, depth):
    hi, lo = split(value)
    t_hi, t_lo = table[:depth, :], table[depth:, :]
    return dot(hi, t_hi) + dot(lo, t_hi) + dot(hi, t_lo)


def table_times(table, value, dims=((1,), (0,))):
    depth = table.shape[1] // 2
    hi, lo = split(value)
    t_hi, t_lo = table[:, :depth], table[:, depth:]
    return dot(t_hi, hi, dims) + dot(t_hi, lo, dims) + dot(t_lo, hi, dims)


def call(body, out, scratch=(), limit=24, flops=2_000_000_000, bytes_accessed=6_000_000):
    return pl.pallas_call(
        body,
        out_shape=out,
        scratch_shapes=list(scratch),
        compiler_params=pltpu.CompilerParams(vmem_limit_bytes=limit << 20),
        cost_estimate=pl.CostEstimate(flops=flops, bytes_accessed=bytes_accessed, transcendentals=0),
    )


def forward_rows(x_ref, wide_ref, tw_ref, whole_ref, tail_ref, out_ref, mid):
    def groups(step, carry):
        base = pl.multiple_of(step * 16, 16)
        left = [x_ref[c, pl.ds(base, 8), h * 128 : h * 128 + 128] for c in range(8) for h in range(8)]
        right = [x_ref[c, pl.ds(base + 8, 8), h * 128 : h * 128 + 128] for c in range(8) for h in range(8)]
        block = jnp.concatenate([jnp.concatenate(left, axis=0), jnp.concatenate(right, axis=0)], axis=1)
        spec = table_times(wide_ref, block)
        for p in range(33):
            cos, sin = tw_ref[p : p + 1, :128], tw_ref[p : p + 1, 128:]
            for g in range(2):
                lanes = slice(g * 128, g * 128 + 128)
                rows = pl.ds(p * 64 + base + g * 8, 8)
                real = spec[p * 8 : p * 8 + 8, lanes]
                if p == 0:
                    mid[rows, :128] = real
                    continue
                if p == 32:
                    mid[rows, :128] = real * cos
                    mid[rows, 128:] = -(real * sin)
                    continue
                imag = spec[(32 + p) * 8 : (32 + p) * 8 + 8, lanes]
                mid[rows, :128] = real * cos + imag * sin
                mid[rows, 128:] = imag * cos - real * sin
        return carry

    lax.fori_loop(0, 4, groups, 0)

    def store(t, value):
        for u in range(2):
            lanes = slice(u * 128, u * 128 + 128)
            out_ref[pl.ds(2 * t + u, 128, stride=32), :] = value[:128, lanes]
            out_ref[pl.ds(16 + 2 * t + u, 128, stride=32), :] = value[128:, lanes]

    for t in range(7):
        rows = mid[(4 * t + 1) * 64 : (4 * t + 5) * 64, :]
        store(t, table_times(whole_ref, rows, ((1,), (1,))))
    plain = jnp.concatenate(
        [mid[29 * 64 : 32 * 64, :], jnp.zeros((192, 384), F32)], axis=1
    )
    mixed = jnp.concatenate(
        [jnp.zeros((64, 256), F32), mid[32 * 64 : 33 * 64, :], mid[0:64, :128]], axis=1
    )
    store(7, table_times(tail_ref, jnp.concatenate([plain, mixed], axis=0), ((1,), (1,))))


def columns(x_ref, w_ref, tw_ref, long_ref, short_ref, ilong_ref, ishort_ref, out_ref):
    cos, sin = tw_ref[:, :128], tw_ref[:, 128:]

    def back(real, imag):
        joint = jnp.concatenate([real, imag], axis=1)
        mixed = times_table(joint, ishort_ref, 256)
        real, imag = mixed[:, :128], mixed[:, 128:]
        return real * cos - imag * sin, imag * cos + real * sin

    def last(real, imag):
        return table_times(ilong_ref, jnp.concatenate([real, imag], axis=0))

    def pair(t, extra):
        blocks = [2 * t, 2 * t + 1]
        real = jnp.concatenate([x_ref[pl.ds(b, 128, stride=32), :] for b in blocks], axis=1)
        imag = jnp.concatenate([x_ref[pl.ds(16 + b, 128, stride=32), :] for b in blocks], axis=1)
        mid = table_times(long_ref, jnp.concatenate([real, imag], axis=0))
        reals, imags = [], []
        tail = None
        for u, b in enumerate(blocks):
            lanes = slice(u * 128, u * 128 + 128)
            real, imag = mid[:128, lanes], mid[128:, lanes]
            joint = jnp.concatenate([real * cos + imag * sin, imag * cos - real * sin], axis=1)
            spec = times_table(joint, short_ref, 256)
            if extra and u == 1:
                weight = w_ref[16]
                tail = back(spec[:, :128] * weight, spec[:, 128:] * weight)
            weight = w_ref[b]
            real, imag = back(spec[:, :128] * weight, spec[:, 128:] * weight)
            reals.append(real)
            imags.append(imag)
        done = last(jnp.concatenate(reals, axis=1), jnp.concatenate(imags, axis=1))
        for u, b in enumerate(blocks):
            lanes = slice(u * 128, u * 128 + 128)
            out_ref[pl.ds(b, 128, stride=32), :] = done[:128, lanes]
            out_ref[pl.ds(16 + b, 128, stride=32), :] = done[128:, lanes]
        if extra:
            done = last(*tail)
            out_ref[pl.ds(31, 128, stride=32), :] = done[128:, :]

    def step(t, carry):
        pair(t, False)
        return carry

    lax.fori_loop(0, 7, step, 0)
    pair(7, True)


def inverse_rows(x_ref, wide_ref, tw_ref, whole_ref, tail_ref, out_ref, mid):
    def product(blocks, tables):
        real = jnp.concatenate([x_ref[pl.ds(b, 128, stride=32), :] for b in blocks], axis=1)
        imag = jnp.concatenate([x_ref[pl.ds(16 + b, 128, stride=32), :] for b in blocks], axis=1)
        joint = jnp.concatenate([real, imag], axis=0).T
        return [table_right(joint, table) for table in tables]

    def table_right(joint, table):
        half = table.shape[1] // 2
        hi, lo = split(joint)
        t_hi, t_lo = table[:, :half], table[:, half:]
        return dot(hi, t_hi) + dot(lo, t_hi) + dot(hi, t_lo)

    def place(p, value):
        cos, sin = tw_ref[p : p + 1, :128], tw_ref[p : p + 1, 128:]
        real, imag = value[:, :128], value[:, 128:256]
        mid[p * 64 : p * 64 + 64, :] = real * cos - imag * sin
        if p < 32:
            mid[(32 + p) * 64 : (33 + p) * 64, :] = imag * cos + real * sin

    for t in range(8):
        tables = [whole_ref] if t < 7 else [whole_ref, tail_ref]
        results = product([2 * t, 2 * t + 1], tables)
        for k in range(4):
            slot = 4 * t + k
            if slot < 31:
                place(slot + 1, results[0][k * 64 : k * 64 + 64, :])
            else:
                value = results[1][k * 64 : k * 64 + 64, :]
                place(32, value)
                mid[0:64, :] = value[:, 256:]

    def groups(step, carry):
        base = pl.multiple_of(step * 16, 16)
        left = [mid[pl.ds(pp * 64 + base, 8), :] for pp in range(64)]
        right = [mid[pl.ds(pp * 64 + base + 8, 8), :] for pp in range(64)]
        block = jnp.concatenate([jnp.concatenate(left, axis=0), jnp.concatenate(right, axis=0)], axis=1)
        field = table_times(wide_ref, block)
        for c in range(8):
            for h in range(8):
                row = (c * 8 + h) * 8
                for g in range(2):
                    out_ref[c, pl.ds(base + g * 8, 8), h * 128 : h * 128 + 128] = field[
                        row : row + 8, g * 128 : g * 128 + 128
                    ]
        return carry

    lax.fori_loop(0, 4, groups, 0)


def reversal():
    flip = np.zeros((128, 128), np.float32)
    for k in range(1, 128):
        flip[k, 128 - k] = 1.0
    first = np.zeros((128, 128), np.float32)
    first[0, 0] = 1.0
    return np.concatenate([flip, first], axis=1).astype(ml_dtypes.bfloat16)


def weights(d_ref, amp_ref, mir_ref, row_ref, flip_ref, out_ref, own, rev, zero):
    d = d_ref[0]
    low = d < 64
    middle = d == 64

    def fill(kb):
        lanes = slice(kb * 128, kb * 128 + 128)
        return amp_ref[:, lanes], mir_ref[:, lanes], row_ref[0:1, lanes]

    for kb in range(64):
        amp, mir, row = fill(kb)
        own_tail = jnp.where(low, amp[32:33], amp[0:1])
        mir_tail = jnp.where(low, mir[0:1], jnp.where(middle, amp[0:1], row))
        flipped = [mir[31 - s : 32 - s] for s in range(31)]
        own_rows = jnp.concatenate(
            [amp[1:32], own_tail, jnp.where(middle, row, own_tail)], axis=0
        )
        mir_rows = jnp.concatenate(flipped + [mir_tail, jnp.where(middle, row, mir_tail)], axis=0)
        own[pl.ds(kb, 33, stride=64), :] = own_rows
        rev[pl.ds(63 - kb, 33, stride=64), :] = mir_rows
        zero[pl.ds((64 - kb) % 64, 33, stride=64), :] = mir_rows

    ka = lax.broadcasted_iota(jnp.int32, (128, 128), 0)
    lane = lax.broadcasted_iota(jnp.int32, (128, 128), 1)
    k0 = ka + 128 * (lane % 64)
    f0 = jnp.where(k0 < N // 2, k0, k0 - N).astype(F32)
    flip, first = flip_ref[:, :128], flip_ref[:, 128:]

    def exact(table, rows):
        a = rows.astype(BF)
        rest = rows - a.astype(F32)
        b = rest.astype(BF)
        c = (rest - b.astype(F32)).astype(BF)
        dims = ((1,), (1,))
        return dot(table, a, dims) + dot(table, b, dims) + dot(table, c, dims)

    def weight(own_rows, rev_rows, zero_rows, p):
        k1 = d * 64 + p
        f1 = jnp.where(k1 < N // 2, k1, k1 - N).astype(F32)
        width_sq = float((N // 128) * (N // 128))
        envelope = 1.0 + bump_height / (1.0 + (f0 * f0 + f1 * f1) / width_sq)
        both = own_rows.T + exact(flip, rev_rows) + exact(first, zero_rows)
        return both * (envelope * (0.5 / (N * N)))

    def step(b, carry):
        rows = pl.ds(pl.multiple_of(b * 128, 128), 128)
        slot = 2 * b + lane // 64
        p = jnp.where(slot < 31, slot + 1, jnp.where(low, 32, 0))
        out_ref[b] = weight(own[rows, :], rev[rows, :], zero[rows, :], p)
        return carry

    lax.fori_loop(0, 16, step, 0)
    upper = slice(31 * 64, 33 * 64)
    p = jnp.where(low, 32, jnp.where(middle, -64 * 64, 0))
    p = jnp.where(lane < 64, jnp.where(low, 32, 0), p)
    value = weight(own[upper, :], rev[upper, :], zero[upper, :], p)
    out_ref[16] = jnp.where(lane < 64, out_ref[15], value)


def catchment_rows(catch_id, owner_map, devices):
    owners = owner_map[:, 0]
    hits = (owners[:, None] == jnp.arange(devices, dtype=jnp.int32)[None, :]).astype(jnp.int32)
    ranks = jnp.sum(hits * (jnp.cumsum(hits, axis=0) - 1), axis=1)
    slot = owners * CAP + ranks
    matches = catch_id.reshape(-1)[:, None] == jnp.arange(owners.shape[0], dtype=jnp.int32)[None, :]
    return jnp.sum(jnp.where(matches, slot[None, :], 0), axis=1)


def shards(white_noise, amplitude, state_prev, catch_id, owner_map, unit_graph, queue_prev):
    d = lax.axis_index(BOTH)
    flat = jax.ShapeDtypeStruct((DEV * 32, 128), F32)
    slab = lax.all_to_all(white_noise.reshape(8, 64, 1024), "col", 0, 0, tiled=True)
    mirrored = lax.ppermute(amplitude[32:64], BOTH, [(i, DEV - 1 - i) for i in range(DEV)])
    partner = lax.ppermute(
        amplitude[0:1], BOTH, [(0, 64)] + [(i, DEV - i) for i in range(1, 64)]
    )
    weight = pl.pallas_call(
        weights,
        out_shape=jax.ShapeDtypeStruct((17, 128, 128), F32),
        in_specs=[pl.BlockSpec(memory_space=pltpu.SMEM)] + [pl.BlockSpec(memory_space=pltpu.VMEM)] * 4,
        scratch_shapes=[pltpu.VMEM((33 * 64, 128), F32)] * 3,
        compiler_params=pltpu.CompilerParams(vmem_limit_bytes=24 << 20),
        cost_estimate=pl.CostEstimate(flops=200_000_000, bytes_accessed=6_000_000, transcendentals=0),
    )(d.astype(jnp.int32).reshape(1), amplitude, mirrored, partner, reversal())

    tw_row = row_twiddle()
    whole, tail = row_forward()
    spec = call(forward_rows, flat, [pltpu.VMEM((33 * 64, 256), F32)])(
        slab, real_forward(), tw_row, whole, tail
    )
    spec = lax.all_to_all(spec.reshape(DEV, 32, 128), BOTH, 0, 0, tiled=True)
    long, short = col_tables(-1.0)
    ilong, ishort = col_tables(1.0)
    stack = lambda table: np.concatenate([table[:, :256], table[:, 256:]], axis=0)
    shaped = call(columns, flat)(
        spec.reshape(DEV * 32, 128), weight, col_twiddle(), long, stack(short), ilong, stack(ishort)
    )
    shaped = lax.all_to_all(shaped.reshape(DEV, 32, 128), BOTH, 0, 0, tiled=True)
    whole, tail = row_inverse()
    field = call(
        inverse_rows, jax.ShapeDtypeStruct((8, 64, 1024), F32), [pltpu.VMEM((64 * 64, 128), F32)]
    )(shaped.reshape(DEV * 32, 128), real_inverse(), tw_row, whole, tail)
    filtered = lax.all_to_all(field, "col", 0, 0, tiled=True).reshape(512, 1024)

    state_new = persist * state_prev + innovate * filtered
    rain = jnp.exp(log_mean + log_scale * state_new)
    tile_rain = rain.reshape(4, TILE, 8, TILE).mean(axis=(1, 3)).reshape(-1)
    tile_slot = catchment_rows(catch_id, owner_map, DEV)
    slot_hits = tile_slot[:, None] == jnp.arange(DEV * CAP, dtype=jnp.int32)[None, :]
    partial_sums = jnp.sum(jnp.where(slot_hits, tile_rain[:, None], 0.0), axis=0)
    received = lax.all_to_all(partial_sums.reshape(DEV, 1, CAP), BOTH, 0, 0, tiled=True)
    slot_rain = received.sum(axis=(0, 1))
    shifted = jnp.concatenate(
        [queue_prev[1:], jnp.zeros((1, queue_prev.shape[1]), jnp.float32)], axis=0
    )
    flow_queue = shifted + unit_graph * slot_rain[None, :]
    return (state_new, flow_queue)


def solution(mesh):
    return jax.shard_map(
        shards,
        mesh=mesh,
        in_specs=(
            P("row", "col"),
            P(BOTH, None),
            P("row", "col"),
            P("row", "col"),
            P(),
            P(None, BOTH),
            P(None, BOTH),
        ),
        out_specs=(P("row", "col"), P(None, BOTH)),
        check_vma=False,
    )
```

```python
from functools import partial

import jax
import jax.numpy as jnp
import ml_dtypes
import numpy as np
from jax import lax
from jax.experimental import pallas as pl
from jax.experimental.pallas import tpu as pltpu
from jax.sharding import PartitionSpec as P

TILE = 128
CAP = 32
N = 8192
DEV = 128
HALF = 32
BOTH = ("row", "col")

bump_height = 64.0
persist = 0.8
innovate = 0.6
log_mean = -0.3
log_scale = 0.6

BF = jnp.bfloat16
F32 = jnp.float32


def hi_lo(table):
    table = np.asarray(table, np.float64)
    hi = table.astype(ml_dtypes.bfloat16)
    lo = (table - hi.astype(np.float64)).astype(ml_dtypes.bfloat16)
    return np.concatenate([hi, lo], axis=1)


def stacked(table):
    half = table.shape[1] // 2
    return np.concatenate([table[:, :half], table[:, half:]], axis=0)


def angle(left, right, length):
    return 2.0 * np.pi / length * (np.outer(left, right) % length)


def real_forward():
    turn = angle(np.arange(64), np.arange(64), 64)
    table = np.concatenate([np.cos(turn[:33]), -np.sin(turn[1:32])], axis=0)
    return hi_lo(table)


def real_inverse():
    turn = angle(np.arange(64), np.arange(64), 64)
    real = 2.0 * np.cos(turn[:, :33])
    real[:, 0] = 1.0
    table = np.concatenate([real, -2.0 * np.sin(turn[:, 1:32])], axis=1)
    return hi_lo(table)


def widen(small_ref, fwd_ref, inv_ref):
    tall = (
        lax.broadcasted_iota(jnp.int32, (512, 64), 0) // 8 == lax.broadcasted_iota(jnp.int32, (512, 64), 1)
    ).astype(BF)
    row = lax.broadcasted_iota(jnp.int32, (512, 512), 0)
    col = lax.broadcasted_iota(jnp.int32, (512, 512), 1)
    same = row % 8 == col % 8
    for k, ref in enumerate([fwd_ref, inv_ref]):
        for half in range(2):
            small = small_ref[k, :, half * 64 : half * 64 + 64]
            grown = dot(dot(tall, small).astype(BF), tall, ((1,), (1,)))
            ref[half * 512 : half * 512 + 512, :] = jnp.where(same, grown, 0.0).astype(BF)


def row_twiddle():
    turn = angle(np.arange(33), np.arange(128), N)
    return np.concatenate([np.cos(turn), np.sin(turn)], axis=1).astype(np.float32)


def row_tables():
    turn = angle(np.arange(128), np.arange(128), 128)
    cos, sin = np.cos(turn), np.sin(turn)
    high = (np.arange(128) >= 64).astype(np.float64)[:, None]
    imag = -sin * high
    imag[64] = 1.0
    forward = np.concatenate([cos * high, imag], axis=0)
    top, bottom = 2.0 * cos * high, -2.0 * sin * high
    top[64] = cos[64]
    bottom[64] = 1.0
    inverse = np.concatenate([top, bottom], axis=0)
    return hi_lo(np.block([[cos, sin], [-sin, cos]])), hi_lo(forward), hi_lo(inverse)


def col_tables(sign):
    turn = angle(np.arange(128), np.arange(128), 128)
    cos, sin = np.cos(turn), sign * np.sin(turn)
    long = np.block([[cos, -sin], [sin, cos]])
    turn = angle(np.arange(64), np.arange(64), 64)
    cos, sin = np.kron(np.eye(2), np.cos(turn)), np.kron(np.eye(2), sign * np.sin(turn))
    short = np.block([[cos, sin], [-sin, cos]])
    return hi_lo(long), hi_lo(short)


def col_twiddle():
    turn = angle(np.arange(128), np.arange(128) % 64, N)
    return np.concatenate([np.cos(turn), np.sin(turn)], axis=1).astype(np.float32)


def split(value):
    hi = value.astype(BF)
    return hi, (value - hi.astype(F32)).astype(BF)


def dot(left, right, dims=((1,), (0,))):
    return lax.dot_general(left, right, (dims, ((), ())), preferred_element_type=F32)


def times_table(value, table):
    rows, half = value.shape[0], table.shape[1] // 2
    hi, lo = split(value)
    first = dot(jnp.concatenate([hi, lo], axis=0), table[:, :half])
    return first[:rows] + first[rows:] + dot(hi, table[:, half:])


def table_times(table, value, dims=((1,), (0,))):
    rows = table.shape[0] // 2
    hi, lo = split(value)
    first = dot(table[...], hi, dims)
    return first[:rows] + first[rows:] + dot(table[:rows, :], lo, dims)


def take(ref, group):
    return jnp.swapaxes(ref[:, group * 8 : group * 8 + 8, :], 0, 1)


def put(ref, group, blocks):
    ref[:, group * 8 : group * 8 + 8, :] = jnp.swapaxes(jnp.stack(blocks), 0, 1)


def call(body, out, scratch=(), limit=24, flops=2_000_000_000, bytes_accessed=6_000_000):
    return pl.pallas_call(
        body,
        out_shape=out,
        scratch_shapes=list(scratch),
        compiler_params=pltpu.CompilerParams(vmem_limit_bytes=limit << 20),
        cost_estimate=pl.CostEstimate(flops=flops, bytes_accessed=bytes_accessed, transcendentals=0),
    )


def forward_rows(x_ref, wide_ref, tw_ref, whole_ref, last_ref, out_ref, mid):
    def groups(step, carry):
        base = pl.multiple_of(step * 16, 16)
        left = [x_ref[c, pl.ds(base, 8), h * 128 : h * 128 + 128] for c in range(8) for h in range(8)]
        right = [x_ref[c, pl.ds(base + 8, 8), h * 128 : h * 128 + 128] for c in range(8) for h in range(8)]
        block = jnp.concatenate([jnp.concatenate(left, axis=0), jnp.concatenate(right, axis=0)], axis=1)
        spec = table_times(wide_ref, block)
        for p in range(33):
            cos, sin = tw_ref[p : p + 1, :128], tw_ref[p : p + 1, 128:]
            for g in range(2):
                lanes = slice(g * 128, g * 128 + 128)
                rows = pl.ds(p * 64 + base + g * 8, 8)
                real = spec[p * 8 : p * 8 + 8, lanes]
                if p == 0:
                    mid[rows, :128] = real
                    continue
                if p == 32:
                    mid[rows, :128] = real * cos
                    mid[rows, 128:] = -(real * sin)
                    continue
                imag = spec[(32 + p) * 8 : (32 + p) * 8 + 8, lanes]
                mid[rows, :128] = real * cos + imag * sin
                mid[rows, 128:] = imag * cos - real * sin
        return carry

    lax.fori_loop(0, 4, groups, 0)

    reals, imags = [], []
    for t in range(8):
        rows = mid[(4 * t + 1) * 64 : (4 * t + 5) * 64, :]
        value = table_times(whole_ref, rows, ((1,), (1,)))
        if t == 7:
            rows = jnp.concatenate([jnp.zeros((192, 128), F32), mid[0:64, :128]], axis=0)
            other = table_times(last_ref, rows, ((1,), (1,)))
            q = lax.broadcasted_iota(jnp.int32, (256, 256), 0) % 128
            lane = lax.broadcasted_iota(jnp.int32, (256, 256), 1)
            value = jnp.where((q >= 64) & (lane >= 192), other, value)
        for u in range(2):
            reals.append(value[:128, u * 128 : u * 128 + 128])
            imags.append(value[128:, u * 128 : u * 128 + 128])
        if t % 4 == 3:
            put(out_ref, t // 4, reals)
            put(out_ref, 2 + t // 4, imags)
            reals, imags = [], []


def columns(x_ref, w_ref, tw_ref, table_ref, out_ref):
    long_ref, ilong_ref = table_ref.at[0:512, :], table_ref.at[512:1024, :]
    short_ref, ishort_ref = [
        jnp.concatenate([table_ref[k : k + 256, :], table_ref[k + 256 : k + 512, :]], axis=1)
        for k in (1024, 1536)
    ]
    cos, sin = tw_ref[:, :128], tw_ref[:, 128:]

    def some(blocks, extra):
        group = blocks[0] // 8
        real = jnp.concatenate(list(take(x_ref, group)), axis=1)
        imag = jnp.concatenate(list(take(x_ref, 2 + group)), axis=1)
        mid = table_times(long_ref, jnp.concatenate([real, imag], axis=0))
        joints = []
        for u in range(len(blocks)):
            real, imag = mid[:128, u * 128 : u * 128 + 128], mid[128:, u * 128 : u * 128 + 128]
            joints.append(jnp.concatenate([real * cos + imag * sin, imag * cos - real * sin], axis=1))
        spec = times_table(jnp.concatenate(joints, axis=0), short_ref)
        joints = []
        for u, b in enumerate(blocks):
            weight = w_ref[b]
            joints.append(spec[u * 128 : u * 128 + 128] * jnp.concatenate([weight, weight], axis=1))
        if extra:
            weight = w_ref[16]
            u = len(blocks) - 1
            joints.append(spec[u * 128 : u * 128 + 128] * jnp.concatenate([weight, weight], axis=1))
        mixed = times_table(jnp.concatenate(joints, axis=0), ishort_ref)
        reals, imags = [], []
        for u in range(len(joints)):
            real, imag = mixed[u * 128 : u * 128 + 128, :128], mixed[u * 128 : u * 128 + 128, 128:]
            reals.append(real * cos - imag * sin)
            imags.append(imag * cos + real * sin)
        done = table_times(
            ilong_ref,
            jnp.concatenate([jnp.concatenate(reals, axis=1), jnp.concatenate(imags, axis=1)], axis=0),
        )
        last = len(joints) - 1
        put(out_ref, group, [done[:128, u * 128 : u * 128 + 128] for u in range(8)])
        put(out_ref, 2 + group, [done[128:, u * 128 : u * 128 + 128] for u in [*range(7), last]])

    some(range(8), False)
    some(range(8, 16), True)


def inverse_rows(x_ref, wide_ref, tw_ref, whole_ref, last_ref, out_ref, mid):

    def place(p, value):
        cos, sin = tw_ref[p : p + 1, :128], tw_ref[p : p + 1, 128:]
        real, imag = value[:, :128], value[:, 128:]
        mid[p * 64 : p * 64 + 64, :] = real * cos - imag * sin
        if p < 32:
            mid[(32 + p) * 64 : (33 + p) * 64, :] = imag * cos + real * sin

    for t in range(8):
        if t % 4 == 0:
            reals, imags = take(x_ref, t // 4), take(x_ref, 2 + t // 4)
        u = t % 4 * 2
        real = jnp.concatenate([reals[u], reals[u + 1]], axis=1)
        imag = jnp.concatenate([imags[u], imags[u + 1]], axis=1)
        joint = jnp.concatenate([real, imag], axis=0).T
        if t == 7:
            slot = lax.broadcasted_iota(jnp.int32, (256, 256), 0)
            q = lax.broadcasted_iota(jnp.int32, (256, 256), 1) % 128
            mid[0:64, :] = times_table(joint[192:, :], last_ref)
            joint = jnp.where((slot >= 192) & (q >= 64), 0.0, joint)
        result = times_table(joint, whole_ref)
        for k in range(4):
            place(4 * t + k + 1, result[k * 64 : k * 64 + 64, :])

    def groups(step, carry):
        base = pl.multiple_of(step * 16, 16)
        left = [mid[pl.ds(pp * 64 + base, 8), :] for pp in range(64)]
        right = [mid[pl.ds(pp * 64 + base + 8, 8), :] for pp in range(64)]
        block = jnp.concatenate([jnp.concatenate(left, axis=0), jnp.concatenate(right, axis=0)], axis=1)
        field = table_times(wide_ref, block)
        for c in range(8):
            for h in range(8):
                row = (c * 8 + h) * 8
                for g in range(2):
                    out_ref[c, pl.ds(base + g * 8, 8), h * 128 : h * 128 + 128] = field[
                        row : row + 8, g * 128 : g * 128 + 128
                    ]
        return carry

    lax.fori_loop(0, 4, groups, 0)


def finish(slot_ref, field_ref, prev_ref, state_ref, sums_ref, cells):
    for block in range(8):
        for h in range(8):
            lanes = slice(h * 128, h * 128 + 128)
            state = persist * prev_ref[block, :, lanes] + innovate * field_ref[block, :, lanes]
            state_ref[block, :, lanes] = state
            rain = jnp.exp(log_mean + log_scale * state)
            cells[h, block : block + 1, :] = jnp.sum(rain, axis=0, keepdims=True)
    dest = lax.broadcasted_iota(jnp.int32, (DEV, 128), 0) * CAP
    lane = lax.broadcasted_iota(jnp.int32, (DEV, 128), 1)
    place = jnp.where(lane < CAP, dest + lane, -1)
    total = jnp.zeros((DEV, 128), F32)
    for h in range(8):
        half = jnp.sum(cells[h], axis=1, keepdims=True)
        for a in range(4):
            tile = (half[2 * a : 2 * a + 1] + half[2 * a + 1 : 2 * a + 2]) * (1.0 / (TILE * TILE))
            total = total + jnp.where(place == slot_ref[a * 8 + h], tile, 0.0)
    sums_ref[...] = total


def reversal():
    flip = np.zeros((128, 128), np.float32)
    for k in range(1, 128):
        flip[k, 128 - k] = 1.0
    first = np.zeros((128, 128), np.float32)
    first[0, 0] = 1.0
    return np.concatenate([flip, first], axis=1).astype(ml_dtypes.bfloat16)


def weights(d_ref, amp_ref, near_ref, far_ref, row_ref, flip_ref, out_ref, own, rev, zero):
    d = d_ref[0]
    low = d < 64
    middle = d == 64

    def fill(kb):
        lanes = slice(kb * 128, kb * 128 + 128)
        return amp_ref[:, lanes], jnp.concatenate([near_ref[:, lanes], far_ref[:, lanes]], axis=0), row_ref[0:1, lanes]

    for kb in range(64):
        amp, mir, row = fill(kb)
        own_tail = jnp.where(low, amp[32:33], amp[0:1])
        mir_tail = jnp.where(low, mir[0:1], jnp.where(middle, amp[0:1], row))
        flipped = [mir[31 - s : 32 - s] for s in range(31)]
        own_rows = jnp.concatenate(
            [amp[1:32], own_tail, jnp.where(middle, row, own_tail)], axis=0
        )
        mir_rows = jnp.concatenate(flipped + [mir_tail, jnp.where(middle, row, mir_tail)], axis=0)
        own[pl.ds(kb, 33, stride=64), :] = own_rows
        rev[pl.ds(63 - kb, 33, stride=64), :] = mir_rows
        zero[pl.ds((64 - kb) % 64, 33, stride=64), :] = mir_rows

    ka = lax.broadcasted_iota(jnp.int32, (128, 128), 0)
    lane = lax.broadcasted_iota(jnp.int32, (128, 128), 1)
    k0 = ka + 128 * (lane % 64)
    f0 = jnp.where(k0 < N // 2, k0, k0 - N).astype(F32)
    flip, first = flip_ref[:, :128], flip_ref[:, 128:]

    def exact(table, rows):
        a = rows.astype(BF)
        rest = rows - a.astype(F32)
        b = rest.astype(BF)
        c = (rest - b.astype(F32)).astype(BF)
        dims = ((1,), (1,))
        return dot(table, a, dims) + dot(table, b, dims) + dot(table, c, dims)

    def weight(own_rows, rev_rows, zero_rows, p):
        k1 = d * 64 + p
        f1 = jnp.where(k1 < N // 2, k1, k1 - N).astype(F32)
        width_sq = float((N // 128) * (N // 128))
        envelope = 1.0 + bump_height / (1.0 + (f0 * f0 + f1 * f1) / width_sq)
        both = own_rows.T + exact(flip, rev_rows) + exact(first, zero_rows)
        return both * (envelope * (0.5 / (N * N)))

    def step(b, carry):
        rows = pl.ds(pl.multiple_of(b * 128, 128), 128)
        slot = 2 * b + lane // 64
        p = jnp.where(slot < 31, slot + 1, jnp.where(low, 32, 0))
        out_ref[b] = weight(own[rows, :], rev[rows, :], zero[rows, :], p)
        return carry

    lax.fori_loop(0, 16, step, 0)
    upper = slice(31 * 64, 33 * 64)
    p = jnp.where(low, 32, jnp.where(middle, -64 * 64, 0))
    p = jnp.where(lane < 64, jnp.where(low, 32, 0), p)
    value = weight(own[upper, :], rev[upper, :], zero[upper, :], p)
    out_ref[16] = jnp.where(lane < 64, out_ref[15], value)


def catchment_rows(catch_id, owner_map, devices):
    owners = owner_map[:, 0]
    hits = (owners[:, None] == jnp.arange(devices, dtype=jnp.int32)[None, :]).astype(jnp.int32)
    ranks = jnp.sum(hits * (jnp.cumsum(hits, axis=0) - 1), axis=1)
    slot = owners * CAP + ranks
    matches = catch_id.reshape(-1)[:, None] == jnp.arange(owners.shape[0], dtype=jnp.int32)[None, :]
    return jnp.sum(jnp.where(matches, slot[None, :], 0), axis=1)


def shards(white_noise, amplitude, state_prev, catch_id, owner_map, unit_graph, queue_prev):
    d = lax.axis_index(BOTH)
    flat = jax.ShapeDtypeStruct((DEV, 32, 128), F32)
    slab = lax.all_to_all(white_noise.reshape(8, 64, 1024), "col", 0, 0, tiled=True)
    forward_wide, inverse_wide = call(
        widen, [jax.ShapeDtypeStruct((1024, 512), BF)] * 2, flops=100_000_000, bytes_accessed=2_000_000
    )(np.stack([real_forward(), real_inverse()]))
    near = lax.ppermute(amplitude[32:48], BOTH, [(i, DEV - 1 - i) for i in range(DEV)])
    far = lax.ppermute(amplitude[48:64], "row", [(i, 15 - i) for i in range(16)])
    partner = lax.ppermute(
        amplitude[0:1], BOTH, [(0, 64)] + [(i, DEV - i) for i in range(1, 64)]
    )
    slab, near, far, partner = lax.optimization_barrier((slab, near, far, partner))
    far = lax.ppermute(far, "col", [(i, 7 - i) for i in range(8)])
    weight = pl.pallas_call(
        weights,
        out_shape=jax.ShapeDtypeStruct((17, 128, 128), F32),
        in_specs=[pl.BlockSpec(memory_space=pltpu.SMEM)] + [pl.BlockSpec(memory_space=pltpu.VMEM)] * 5,
        scratch_shapes=[pltpu.VMEM((33 * 64, 128), F32)] * 3,
        compiler_params=pltpu.CompilerParams(vmem_limit_bytes=24 << 20),
        cost_estimate=pl.CostEstimate(flops=200_000_000, bytes_accessed=6_000_000, transcendentals=0),
    )(d.astype(jnp.int32).reshape(1), amplitude, near, far, partner, reversal())

    tw_row = row_twiddle()
    whole, forward_last, inverse_last = row_tables()
    spec = call(forward_rows, flat, [pltpu.VMEM((33 * 64, 256), F32)])(
        slab, forward_wide, tw_row, stacked(whole), stacked(forward_last)
    )
    spec, far = lax.optimization_barrier((spec, far))
    spec = lax.all_to_all(spec, BOTH, 0, 0, tiled=True)
    long, short = col_tables(-1.0)
    ilong, ishort = col_tables(1.0)
    tables = np.concatenate([stacked(table) for table in (long, ilong, short, ishort)], axis=0)
    shaped = call(columns, flat)(spec, weight, col_twiddle(), tables)
    shaped = lax.all_to_all(shaped, BOTH, 0, 0, tiled=True)
    slab_type = jax.ShapeDtypeStruct((8, 64, 1024), F32)
    field = call(inverse_rows, slab_type, [pltpu.VMEM((64 * 64, 128), F32)])(
        shaped, inverse_wide, tw_row, whole, inverse_last
    )
    filtered = lax.all_to_all(field, "col", 0, 0, tiled=True)
    tile_slot = catchment_rows(catch_id, owner_map, DEV)
    state_new, sums = pl.pallas_call(
        finish,
        out_shape=[slab_type, jax.ShapeDtypeStruct((DEV, 128), F32)],
        in_specs=[pl.BlockSpec(memory_space=pltpu.SMEM)] + [pl.BlockSpec(memory_space=pltpu.VMEM)] * 2,
        scratch_shapes=[pltpu.VMEM((8, 8, 128), F32)],
        compiler_params=pltpu.CompilerParams(vmem_limit_bytes=24 << 20),
        cost_estimate=pl.CostEstimate(flops=5_000_000, bytes_accessed=6_000_000, transcendentals=500_000),
    )(tile_slot.astype(jnp.int32), filtered, state_prev.reshape(8, 64, 1024))
    received = lax.all_to_all(sums.reshape(DEV, 1, 128), BOTH, 0, 0, tiled=True)
    slot_rain = received.sum(axis=(0, 1))[:CAP]
    shifted = jnp.concatenate(
        [queue_prev[1:], jnp.zeros((1, queue_prev.shape[1]), jnp.float32)], axis=0
    )
    flow_queue = shifted + unit_graph * slot_rain[None, :]
    return (state_new.reshape(512, 1024), flow_queue)


def solution(mesh):
    return jax.shard_map(
        shards,
        mesh=mesh,
        in_specs=(
            P("row", "col"),
            P(BOTH, None),
            P("row", "col"),
            P("row", "col"),
            P(),
            P(None, BOTH),
            P(None, BOTH),
        ),
        out_specs=(P("row", "col"), P(None, BOTH)),
        check_vma=False,
    )
```

```python
from functools import partial

import jax
import jax.numpy as jnp
import ml_dtypes
import numpy as np
from jax import lax
from jax.experimental import pallas as pl
from jax.experimental.pallas import tpu as pltpu
from jax.sharding import Mesh
from jax.sharding import PartitionSpec as P

TILE = 128
CAP = 32
N = 8192
DEV = 128
FAR = 8
ROW = ("y", "x")
COL = ("z", "core")
BOTH = ROW + COL
CORES = ("core", "y", "x", "z")
ORDER = [2 * (e % 64) + e // 64 for e in range(DEV)]
PAIRS = ORDER + [DEV + e for e in ORDER]

bump_height = 64.0
persist = 0.8
innovate = 0.6
log_mean = -0.3
log_scale = 0.6

BF = jnp.bfloat16
F32 = jnp.float32


def hi_lo(table):
    table = np.asarray(table, np.float64)
    hi = table.astype(ml_dtypes.bfloat16)
    lo = (table - hi.astype(np.float64)).astype(ml_dtypes.bfloat16)
    return np.concatenate([hi, lo], axis=1)


def stacked(table):
    half = table.shape[1] // 2
    return np.concatenate([table[:, :half], table[:, half:]], axis=0)


def angle(left, right, length):
    return 2.0 * np.pi / length * (np.outer(left, right) % length)


def real_forward():
    turn = angle(np.arange(64), np.arange(64), 64)
    table = np.concatenate([np.cos(turn[:33]), -np.sin(turn[1:32])], axis=0)
    return hi_lo(table)


def real_inverse():
    turn = angle(np.arange(64), np.arange(64), 64)
    real = 2.0 * np.cos(turn[:, :33])
    real[:, 0] = 1.0
    table = np.concatenate([real, -2.0 * np.sin(turn[:, 1:32])], axis=1)
    return hi_lo(table)


def widen(small_ref, fwd_ref, inv_ref):
    tall = (
        lax.broadcasted_iota(jnp.int32, (512, 64), 0) // 8 == lax.broadcasted_iota(jnp.int32, (512, 64), 1)
    ).astype(BF)
    row = lax.broadcasted_iota(jnp.int32, (512, 512), 0)
    col = lax.broadcasted_iota(jnp.int32, (512, 512), 1)
    same = row % 8 == col % 8
    for k, ref in enumerate([fwd_ref, inv_ref]):
        for half in range(2):
            small = small_ref[k, :, half * 64 : half * 64 + 64]
            grown = dot(dot(tall, small).astype(BF), tall, ((1,), (1,)))
            ref[half * 512 : half * 512 + 512, :] = jnp.where(same, grown, 0.0).astype(BF)


def row_twiddle():
    turn = angle(np.arange(33), np.arange(128), N)
    return np.concatenate([np.cos(turn), np.sin(turn)], axis=1).astype(np.float32)


def row_tables():
    turn = angle(np.arange(128), np.arange(128), 128)
    cos, sin = np.cos(turn), np.sin(turn)
    high = (np.arange(128) >= 64).astype(np.float64)[:, None]
    imag = -sin * high
    imag[64] = 1.0
    forward = np.concatenate([cos * high, imag], axis=0)
    top, bottom = 2.0 * cos * high, -2.0 * sin * high
    top[64] = cos[64]
    bottom[64] = 1.0
    inverse = np.concatenate([top, bottom], axis=0)
    whole = np.block([[cos, sin], [-sin, cos]])
    return [hi_lo(table[PAIRS]) for table in (whole, forward, inverse)]


def col_tables(sign):
    turn = angle(np.arange(128), np.arange(128), 128)
    cos, sin = np.cos(turn), sign * np.sin(turn)
    long = np.block([[cos, -sin], [sin, cos]])
    long = long[:, PAIRS] if sign < 0 else long[PAIRS]
    turn = angle(np.arange(64), np.arange(64), 64)
    cos, sin = np.kron(np.eye(2), np.cos(turn)), np.kron(np.eye(2), sign * np.sin(turn))
    short = np.block([[cos, sin], [-sin, cos]])
    return hi_lo(long), hi_lo(short)


def col_twiddle():
    turn = angle(np.arange(128), np.arange(128) % 64, N)
    return np.concatenate([np.cos(turn), np.sin(turn)], axis=1).astype(np.float32)


def split(value):
    hi = value.astype(BF)
    return hi, (value - hi.astype(F32)).astype(BF)


def dot(left, right, dims=((1,), (0,))):
    return lax.dot_general(left, right, (dims, ((), ())), preferred_element_type=F32)


def times_table(value, table):
    rows, half = value.shape[0], table.shape[1] // 2
    hi, lo = split(value)
    first = dot(jnp.concatenate([hi, lo], axis=0), table[:, :half])
    return first[:rows] + first[rows:] + dot(hi, table[:, half:])


def table_times(table, value, dims=((1,), (0,))):
    rows = table.shape[0] // 2
    hi, lo = split(value)
    first = dot(table[...], hi, dims)
    return first[:rows] + first[rows:] + dot(table[:rows, :], lo, dims)


def take(ref, group):
    return jnp.swapaxes(ref[:, group * 8 : group * 8 + 8, :], 0, 1)


def put(ref, group, blocks):
    ref[:, group * 8 : group * 8 + 8, :] = jnp.swapaxes(jnp.stack(blocks), 0, 1)


def call(body, out, scratch=(), limit=24, flops=2_000_000_000, bytes_accessed=6_000_000):
    return pl.pallas_call(
        body,
        out_shape=out,
        scratch_shapes=list(scratch),
        compiler_params=pltpu.CompilerParams(vmem_limit_bytes=limit << 20),
        cost_estimate=pl.CostEstimate(flops=flops, bytes_accessed=bytes_accessed, transcendentals=0),
    )


def forward_rows(x_ref, wide_ref, tw_ref, whole_ref, last_ref, out_ref, mid):
    def groups(step, carry):
        base = pl.multiple_of(step * 16, 16)
        left = [x_ref[c, pl.ds(base, 8), h * 128 : h * 128 + 128] for c in range(8) for h in range(8)]
        right = [x_ref[c, pl.ds(base + 8, 8), h * 128 : h * 128 + 128] for c in range(8) for h in range(8)]
        block = jnp.concatenate([jnp.concatenate(left, axis=0), jnp.concatenate(right, axis=0)], axis=1)
        spec = table_times(wide_ref, block)
        for p in range(33):
            cos, sin = tw_ref[p : p + 1, :128], tw_ref[p : p + 1, 128:]
            for g in range(2):
                lanes = slice(g * 128, g * 128 + 128)
                rows = pl.ds(p * 64 + base + g * 8, 8)
                real = spec[p * 8 : p * 8 + 8, lanes]
                if p == 0:
                    mid[rows, :128] = real
                    continue
                if p == 32:
                    mid[rows, :128] = real * cos
                    mid[rows, 128:] = -(real * sin)
                    continue
                imag = spec[(32 + p) * 8 : (32 + p) * 8 + 8, lanes]
                mid[rows, :128] = real * cos + imag * sin
                mid[rows, 128:] = imag * cos - real * sin
        return carry

    lax.fori_loop(0, 4, groups, 0)

    reals, imags = [], []
    for t in range(8):
        rows = mid[(4 * t + 1) * 64 : (4 * t + 5) * 64, :]
        value = table_times(whole_ref, rows, ((1,), (1,)))
        if t == 7:
            rows = jnp.concatenate([jnp.zeros((192, 128), F32), mid[0:64, :128]], axis=0)
            other = table_times(last_ref, rows, ((1,), (1,)))
            order = lax.broadcasted_iota(jnp.int32, (256, 256), 0) % 64
            lane = lax.broadcasted_iota(jnp.int32, (256, 256), 1)
            value = jnp.where((order >= 32) & (lane >= 192), other, value)
        for u in range(2):
            reals.append(value[:128, u * 128 : u * 128 + 128])
            imags.append(value[128:, u * 128 : u * 128 + 128])
        if t % 4 == 3:
            put(out_ref, t // 4, reals)
            put(out_ref, 2 + t // 4, imags)
            reals, imags = [], []


def columns(x_ref, far_ref, near_ref, tw_ref, table_ref, out_ref):
    long_ref, ilong_ref = table_ref.at[0:512, :], table_ref.at[512:1024, :]
    short_ref, ishort_ref = [
        jnp.concatenate([table_ref[k : k + 256, :], table_ref[k + 256 : k + 512, :]], axis=1)
        for k in (1024, 1536)
    ]
    cos, sin = tw_ref[:, :128], tw_ref[:, 128:]

    def some(blocks, extra):
        group = blocks[0] // 8
        real = jnp.concatenate(list(take(x_ref, group)), axis=1)
        imag = jnp.concatenate(list(take(x_ref, 2 + group)), axis=1)
        mid = table_times(long_ref, jnp.concatenate([real, imag], axis=0))
        joints = []
        for u in range(len(blocks)):
            real, imag = mid[:128, u * 128 : u * 128 + 128], mid[128:, u * 128 : u * 128 + 128]
            joints.append(jnp.concatenate([real * cos + imag * sin, imag * cos - real * sin], axis=1))
        spec = times_table(jnp.concatenate(joints, axis=0), short_ref)
        joints = []
        for u, b in enumerate(blocks):
            weight = far_ref[b] if b < FAR // 2 else near_ref[b - FAR // 2]
            joints.append(spec[u * 128 : u * 128 + 128] * jnp.concatenate([weight, weight], axis=1))
        if extra:
            weight = near_ref[16 - FAR // 2]
            u = len(blocks) - 1
            joints.append(spec[u * 128 : u * 128 + 128] * jnp.concatenate([weight, weight], axis=1))
        mixed = times_table(jnp.concatenate(joints, axis=0), ishort_ref)
        reals, imags = [], []
        for u in range(len(joints)):
            real, imag = mixed[u * 128 : u * 128 + 128, :128], mixed[u * 128 : u * 128 + 128, 128:]
            reals.append(real * cos - imag * sin)
            imags.append(imag * cos + real * sin)
        done = table_times(
            ilong_ref,
            jnp.concatenate([jnp.concatenate(reals, axis=1), jnp.concatenate(imags, axis=1)], axis=0),
        )
        last = len(joints) - 1
        put(out_ref, group, [done[:128, u * 128 : u * 128 + 128] for u in range(8)])
        put(out_ref, 2 + group, [done[128:, u * 128 : u * 128 + 128] for u in [*range(7), last]])

    some(range(8), False)
    some(range(8, 16), True)


def inverse_rows(x_ref, wide_ref, tw_ref, whole_ref, last_ref, out_ref, mid):

    def place(p, value):
        cos, sin = tw_ref[p : p + 1, :128], tw_ref[p : p + 1, 128:]
        real, imag = value[:, :128], value[:, 128:]
        mid[p * 64 : p * 64 + 64, :] = real * cos - imag * sin
        if p < 32:
            mid[(32 + p) * 64 : (33 + p) * 64, :] = imag * cos + real * sin

    for t in range(8):
        if t % 4 == 0:
            reals, imags = take(x_ref, t // 4), take(x_ref, 2 + t // 4)
        u = t % 4 * 2
        real = jnp.concatenate([reals[u], reals[u + 1]], axis=1)
        imag = jnp.concatenate([imags[u], imags[u + 1]], axis=1)
        joint = jnp.concatenate([real, imag], axis=0).T
        if t == 7:
            slot = lax.broadcasted_iota(jnp.int32, (256, 256), 0)
            order = lax.broadcasted_iota(jnp.int32, (256, 256), 1) % 64
            mid[0:64, :] = times_table(joint[192:, :], last_ref)
            joint = jnp.where((slot >= 192) & (order >= 32), 0.0, joint)
        result = times_table(joint, whole_ref)
        for k in range(4):
            place(4 * t + k + 1, result[k * 64 : k * 64 + 64, :])

    def groups(step, carry):
        base = pl.multiple_of(step * 16, 16)
        left = [mid[pl.ds(pp * 64 + base, 8), :] for pp in range(64)]
        right = [mid[pl.ds(pp * 64 + base + 8, 8), :] for pp in range(64)]
        block = jnp.concatenate([jnp.concatenate(left, axis=0), jnp.concatenate(right, axis=0)], axis=1)
        field = table_times(wide_ref, block)
        for c in range(8):
            for h in range(8):
                row = (c * 8 + h) * 8
                for g in range(2):
                    out_ref[c, pl.ds(base + g * 8, 8), h * 128 : h * 128 + 128] = field[
                        row : row + 8, g * 128 : g * 128 + 128
                    ]
        return carry

    lax.fori_loop(0, 4, groups, 0)


def tile_sums(slot_ref, field_ref, prev_ref, sums_ref, cells):
    for block in range(8):
        for h in range(8):
            lanes = slice(h * 128, h * 128 + 128)
            state = persist * prev_ref[block, :, lanes] + innovate * field_ref[block, :, lanes]
            rain = jnp.exp(log_mean + log_scale * state)
            cells[h, block : block + 1, :] = jnp.sum(rain, axis=0, keepdims=True)
    dest = lax.broadcasted_iota(jnp.int32, (DEV, 128), 0) * CAP
    lane = lax.broadcasted_iota(jnp.int32, (DEV, 128), 1)
    place = jnp.where(lane < CAP, dest + lane, -1)
    total = jnp.zeros((DEV, 128), F32)
    for h in range(8):
        half = jnp.sum(cells[h], axis=1, keepdims=True)
        for a in range(4):
            tile = (half[2 * a : 2 * a + 1] + half[2 * a + 1 : 2 * a + 2]) * (1.0 / (TILE * TILE))
            total = total + jnp.where(place == slot_ref[a * 8 + h], tile, 0.0)
    sums_ref[...] = total


def next_state(field_ref, prev_ref, state_ref):
    state_ref[...] = persist * prev_ref[...] + innovate * field_ref[...]


def reversal():
    flip = np.zeros((128, 128), np.float32)
    for k in range(1, 128):
        flip[k, 128 - k] = 1.0
    first = np.zeros((128, 128), np.float32)
    first[0, 0] = 1.0
    return np.concatenate([np.eye(128, dtype=np.float32), flip, first], axis=1).astype(ml_dtypes.bfloat16)


def exact_parts(rows):
    a = rows.astype(BF)
    rest = rows - a.astype(F32)
    b = rest.astype(BF)
    return a, b, (rest - b.astype(F32)).astype(BF)


def unfold(ref, group, backward):
    order = range(63, -1, -1) if backward else range(64)
    rows = slice(group * 8, group * 8 + 8)
    return jnp.swapaxes(jnp.stack([ref[rows, k * 128 : k * 128 + 128] for k in order]), 0, 1)


def weight_block(own, rev, flip_ref, d, p):
    rows = [
        jnp.concatenate([a, b, pltpu.roll(b, 1, 0)], axis=1) for a, b in zip(own, rev, strict=True)
    ]
    joint = jnp.concatenate(rows, axis=0)
    dims = ((1,), (1,))
    both = sum(dot(flip_ref[...], part, dims) for part in exact_parts(joint))
    shape = (128, len(own) * 64)
    ka = lax.broadcasted_iota(jnp.int32, shape, 0)
    lane = lax.broadcasted_iota(jnp.int32, shape, 1)
    k0 = ka + 128 * (lane % 64)
    f0 = jnp.where(k0 < N // 2, k0, k0 - N).astype(F32)
    k1 = d * 64 + p(lane // 64)
    f1 = jnp.where(k1 < N // 2, k1, k1 - N).astype(F32)
    width_sq = float((N // 128) * (N // 128))
    envelope = 1.0 + bump_height / (1.0 + (f0 * f0 + f1 * f1) / width_sq)
    return both * (envelope * (0.5 / (N * N)))


def put_weight(out_ref, first, value):
    for b in range(value.shape[1] // 128):
        out_ref[first + b] = value[:, b * 128 : b * 128 + 128]


def far_weights(d_ref, amp_ref, far_ref, flip_ref, out_ref):
    d = d_ref[0]
    own = [row for g in range(FAR // 8 + 1) for row in unfold(amp_ref, g, False)]
    rev = [row for g in range(FAR // 8) for row in unfold(far_ref, g, True)]
    for s in range(0, FAR, 8):
        mirrored = [rev[FAR - 1 - k] for k in range(s, s + 8)]
        value = weight_block(own[s + 1 : s + 9], mirrored, flip_ref, d, lambda k, s=s: k + (s + 1))
        put_weight(out_ref, s // 2, value)


def near_weights(d_ref, amp_ref, near_ref, row_ref, flip_ref, out_ref):
    d = d_ref[0]
    low = d < 64
    middle = d == 64
    own = [row for g in range(5) for row in unfold(amp_ref, g, False)]
    rev = [row for g in range(4 - FAR // 8) for row in unfold(near_ref, g, True)]
    row = row_ref[...]
    turn = lax.broadcasted_iota(jnp.int32, (64, 64), 0) + lax.broadcasted_iota(jnp.int32, (64, 64), 1) == 63
    turned = sum(dot(turn.astype(BF), part) for part in exact_parts(row))
    back = unfold(amp_ref, 0, True)[0]
    own_tail = jnp.where(low, own[32], own[0])
    rev_tail = jnp.where(low, rev[0], jnp.where(middle, back, turned))
    own_all = own[1:32] + [own_tail]
    rev_all = [None] * FAR + [rev[31 - k] for k in range(FAR, 31)] + [rev_tail]

    def plain(k, s):
        return jnp.where(k + s < 31, k + (s + 1), jnp.where(low, 32, 0))

    for s in range(FAR, 32, 8):
        value = weight_block(own_all[s : s + 8], rev_all[s : s + 8], flip_ref, d, lambda k, s=s: plain(k, s))
        put_weight(out_ref, (s - FAR) // 2, value)
    value = weight_block(
        [own[31], jnp.where(middle, row, own_tail)],
        [rev[1], jnp.where(middle, turned, rev_tail)],
        flip_ref,
        d,
        lambda k: jnp.where(k == 0, 31, jnp.where(low, 32, jnp.where(middle, -64 * 64, 0))),
    )
    put_weight(out_ref, 16 - FAR // 2, value)


def catchment_rows(catch_id, owner_map, devices):
    owners = owner_map[:, 0]
    hits = (owners[:, None] == jnp.arange(devices, dtype=jnp.int32)[None, :]).astype(jnp.int32)
    ranks = jnp.sum(hits * (jnp.cumsum(hits, axis=0) - 1), axis=1)
    slot = owners * CAP + ranks
    matches = catch_id.reshape(-1)[:, None] == jnp.arange(owners.shape[0], dtype=jnp.int32)[None, :]
    return jnp.sum(jnp.where(matches, slot[None, :], 0), axis=1)


def shards(white_noise, amplitude, state_prev, catch_id, owner_map, unit_graph, queue_prev):
    d = lax.axis_index(BOTH)
    flat = jax.ShapeDtypeStruct((DEV, 32, 128), F32)
    slab = lax.all_to_all(white_noise.reshape(8, 64, 1024), COL, 0, 0, tiled=True)
    small = np.stack([real_forward(), real_inverse()])
    near = lax.ppermute(amplitude[32 : 64 - FAR], BOTH, [(i, DEV - 1 - i) for i in range(DEV)])
    far = lax.ppermute(amplitude[64 - FAR : 64], ROW, [(i, 15 - i) for i in range(16)])
    partner = lax.ppermute(
        amplitude[0:1], BOTH, [(0, 64)] + [(i, DEV - i) for i in range(1, 64)]
    )
    slab, near, far, partner = lax.optimization_barrier((slab, near, far, partner))
    far = lax.ppermute(far, COL, [(i, 7 - i) for i in range(8)])
    forward_wide, inverse_wide = call(
        widen, [jax.ShapeDtypeStruct((1024, 512), BF)] * 2, flops=100_000_000, bytes_accessed=2_000_000
    )(small)
    tile_slot = catchment_rows(catch_id, owner_map, DEV).astype(jnp.int32)
    device = d.astype(jnp.int32).reshape(1)
    scalar, vector = pl.BlockSpec(memory_space=pltpu.SMEM), pl.BlockSpec(memory_space=pltpu.VMEM)

    def weigh(body, blocks, *args):
        return pl.pallas_call(
            body,
            out_shape=jax.ShapeDtypeStruct((blocks, 128, 128), F32),
            in_specs=[scalar] + [vector] * len(args),
            compiler_params=pltpu.CompilerParams(vmem_limit_bytes=24 << 20),
            cost_estimate=pl.CostEstimate(flops=300_000_000, bytes_accessed=3_000_000, transcendentals=0),
        )(device, *args)

    flip = reversal()
    near_weight = weigh(near_weights, 17 - FAR // 2, amplitude, near, partner.reshape(64, 128), flip)
    far_weight = weigh(far_weights, FAR // 2, amplitude, far, flip)

    tw_row = row_twiddle()
    whole, forward_last, inverse_last = row_tables()
    spec = call(forward_rows, flat, [pltpu.VMEM((33 * 64, 256), F32)])(
        slab, forward_wide, tw_row, stacked(whole), stacked(forward_last)
    )
    spec, near_weight, far_weight, tile_slot, inverse_wide = lax.optimization_barrier(
        (spec, near_weight, far_weight, tile_slot, inverse_wide)
    )
    spec = lax.all_to_all(spec, CORES, 0, 0, tiled=True)
    long, short = col_tables(-1.0)
    ilong, ishort = col_tables(1.0)
    tables = np.concatenate([stacked(table) for table in (long, ilong, short, ishort)], axis=0)
    shaped = call(columns, flat)(spec, far_weight, near_weight, col_twiddle(), tables)
    shaped = lax.all_to_all(shaped, CORES, 0, 0, tiled=True)
    slab_type = jax.ShapeDtypeStruct((8, 64, 1024), F32)
    field = call(inverse_rows, slab_type, [pltpu.VMEM((64 * 64, 128), F32)])(
        shaped, inverse_wide, tw_row, whole, inverse_last
    )
    filtered = lax.all_to_all(field, COL, 0, 0, tiled=True)
    prev = state_prev.reshape(8, 64, 1024)
    sums = pl.pallas_call(
        tile_sums,
        out_shape=jax.ShapeDtypeStruct((DEV, 128), F32),
        in_specs=[scalar] + [vector] * 2,
        scratch_shapes=[pltpu.VMEM((8, 8, 128), F32)],
        compiler_params=pltpu.CompilerParams(vmem_limit_bytes=24 << 20),
        cost_estimate=pl.CostEstimate(flops=5_000_000, bytes_accessed=4_000_000, transcendentals=500_000),
    )(tile_slot, filtered, prev)
    state_new = call(next_state, slab_type, flops=2_000_000)(filtered, prev)
    received = lax.all_to_all(sums.reshape(DEV, 1, 128), BOTH, 0, 0, tiled=True)
    slot_rain = received.sum(axis=(0, 1))[:CAP]
    shifted = jnp.concatenate(
        [queue_prev[1:], jnp.zeros((1, queue_prev.shape[1]), jnp.float32)], axis=0
    )
    flow_queue = shifted + unit_graph * slot_rain[None, :]
    return (state_new.reshape(512, 1024), flow_queue)


def solution(mesh):
    chips = Mesh(mesh.devices.reshape(4, 4, 4, 2), BOTH)
    return jax.shard_map(
        shards,
        mesh=chips,
        in_specs=(P(ROW, COL), P(BOTH, None), P(ROW, COL), P(ROW, COL), P(), P(None, BOTH), P(None, BOTH)),
        out_specs=(P(ROW, COL), P(None, BOTH)),
        check_vma=False,
    )
```

```python
from functools import partial

import jax
import jax.numpy as jnp
import ml_dtypes
import numpy as np
from jax import lax
from jax.experimental import pallas as pl
from jax.experimental.pallas import tpu as pltpu
from jax.sharding import PartitionSpec as P

TILE = 128
CAP = 32
N = 8192
DEV = 128
FAR = 8
BOTH = ("row", "col")

bump_height = 64.0
persist = 0.8
innovate = 0.6
log_mean = -0.3
log_scale = 0.6

BF = jnp.bfloat16
F32 = jnp.float32


def hi_lo(table):
    table = np.asarray(table, np.float64)
    hi = table.astype(ml_dtypes.bfloat16)
    lo = (table - hi.astype(np.float64)).astype(ml_dtypes.bfloat16)
    return np.concatenate([hi, lo], axis=1)


def stacked(table):
    half = table.shape[1] // 2
    return np.concatenate([table[:, :half], table[:, half:]], axis=0)


def angle(left, right, length):
    return 2.0 * np.pi / length * (np.outer(left, right) % length)


def real_forward():
    turn = angle(np.arange(64), np.arange(64), 64)
    table = np.concatenate([np.cos(turn[:33]), -np.sin(turn[1:32])], axis=0)
    return hi_lo(table)


def real_inverse():
    turn = angle(np.arange(64), np.arange(64), 64)
    real = 2.0 * np.cos(turn[:, :33])
    real[:, 0] = 1.0
    table = np.concatenate([real, -2.0 * np.sin(turn[:, 1:32])], axis=1)
    return hi_lo(table)


def widen(small_ref, fwd_ref, inv_ref):
    tall = (
        lax.broadcasted_iota(jnp.int32, (512, 64), 0) // 8 == lax.broadcasted_iota(jnp.int32, (512, 64), 1)
    ).astype(BF)
    row = lax.broadcasted_iota(jnp.int32, (512, 512), 0)
    col = lax.broadcasted_iota(jnp.int32, (512, 512), 1)
    same = row % 8 == col % 8
    for k, ref in enumerate([fwd_ref, inv_ref]):
        for half in range(2):
            small = small_ref[k, :, half * 64 : half * 64 + 64]
            grown = dot(dot(tall, small).astype(BF), tall, ((1,), (1,)))
            ref[half * 512 : half * 512 + 512, :] = jnp.where(same, grown, 0.0).astype(BF)


def row_twiddle():
    turn = angle(np.arange(33), np.arange(128), N)
    return np.concatenate([np.cos(turn), np.sin(turn)], axis=1).astype(np.float32)


def row_tables():
    turn = angle(np.arange(128), np.arange(128), 128)
    cos, sin = np.cos(turn), np.sin(turn)
    high = (np.arange(128) >= 64).astype(np.float64)[:, None]
    imag = -sin * high
    imag[64] = 1.0
    forward = np.concatenate([cos * high, imag], axis=0)
    top, bottom = 2.0 * cos * high, -2.0 * sin * high
    top[64] = cos[64]
    bottom[64] = 1.0
    inverse = np.concatenate([top, bottom], axis=0)
    return hi_lo(np.block([[cos, sin], [-sin, cos]])), hi_lo(forward), hi_lo(inverse)


def col_tables(sign):
    turn = angle(np.arange(128), np.arange(128), 128)
    cos, sin = np.cos(turn), sign * np.sin(turn)
    long = np.block([[cos, -sin], [sin, cos]])
    turn = angle(np.arange(64), np.arange(64), 64)
    cos, sin = np.kron(np.eye(2), np.cos(turn)), np.kron(np.eye(2), sign * np.sin(turn))
    short = np.block([[cos, sin], [-sin, cos]])
    return hi_lo(long), hi_lo(short)


def col_twiddle():
    turn = angle(np.arange(128), np.arange(128) % 64, N)
    return np.concatenate([np.cos(turn), np.sin(turn)], axis=1).astype(np.float32)


def split(value):
    hi = value.astype(BF)
    return hi, (value - hi.astype(F32)).astype(BF)


def dot(left, right, dims=((1,), (0,))):
    return lax.dot_general(left, right, (dims, ((), ())), preferred_element_type=F32)


def times_table(value, table):
    rows, half = value.shape[0], table.shape[1] // 2
    hi, lo = split(value)
    first = dot(jnp.concatenate([hi, lo], axis=0), table[:, :half])
    return first[:rows] + first[rows:] + dot(hi, table[:, half:])


def table_times(table, value, dims=((1,), (0,))):
    rows = table.shape[0] // 2
    hi, lo = split(value)
    first = dot(table[...], hi, dims)
    return first[:rows] + first[rows:] + dot(table[:rows, :], lo, dims)


def take(ref, group):
    return jnp.swapaxes(ref[:, group * 8 : group * 8 + 8, :], 0, 1)


def put(ref, group, blocks):
    ref[:, group * 8 : group * 8 + 8, :] = jnp.swapaxes(jnp.stack(blocks), 0, 1)


def call(body, out, scratch=(), limit=24, flops=2_000_000_000, bytes_accessed=6_000_000):
    return pl.pallas_call(
        body,
        out_shape=out,
        scratch_shapes=list(scratch),
        compiler_params=pltpu.CompilerParams(vmem_limit_bytes=limit << 20),
        cost_estimate=pl.CostEstimate(flops=flops, bytes_accessed=bytes_accessed, transcendentals=0),
    )


def forward_rows(x_hbm, wide_hbm, tw_ref, whole_ref, last_ref, out_ref, mid, x_ref, wide_ref, sems):
    def fetch(step):
        rows = pl.ds(pl.multiple_of(step * 16, 16), 16)
        return pltpu.make_async_copy(x_hbm.at[:, rows, :], x_ref.at[:, rows, :], sems.at[step])

    table = pltpu.make_async_copy(wide_hbm, wide_ref, sems.at[4])
    table.start()
    for step in range(4):
        fetch(step).start()
    table.wait()

    def groups(step, carry):
        base = pl.multiple_of(step * 16, 16)
        fetch(step).wait()
        left = [x_ref[c, pl.ds(base, 8), h * 128 : h * 128 + 128] for c in range(8) for h in range(8)]
        right = [x_ref[c, pl.ds(base + 8, 8), h * 128 : h * 128 + 128] for c in range(8) for h in range(8)]
        block = jnp.concatenate([jnp.concatenate(left, axis=0), jnp.concatenate(right, axis=0)], axis=1)
        spec = table_times(wide_ref, block)
        for p in range(33):
            cos, sin = tw_ref[p : p + 1, :128], tw_ref[p : p + 1, 128:]
            for g in range(2):
                lanes = slice(g * 128, g * 128 + 128)
                rows = pl.ds(p * 64 + base + g * 8, 8)
                real = spec[p * 8 : p * 8 + 8, lanes]
                if p == 0:
                    mid[rows, :128] = real
                    continue
                if p == 32:
                    mid[rows, :128] = real * cos
                    mid[rows, 128:] = -(real * sin)
                    continue
                imag = spec[(32 + p) * 8 : (32 + p) * 8 + 8, lanes]
                mid[rows, :128] = real * cos + imag * sin
                mid[rows, 128:] = imag * cos - real * sin
        return carry

    lax.fori_loop(0, 4, groups, 0)

    reals, imags = [], []
    for t in range(8):
        rows = mid[(4 * t + 1) * 64 : (4 * t + 5) * 64, :]
        value = table_times(whole_ref, rows, ((1,), (1,)))
        if t == 7:
            rows = jnp.concatenate([jnp.zeros((192, 128), F32), mid[0:64, :128]], axis=0)
            other = table_times(last_ref, rows, ((1,), (1,)))
            q = lax.broadcasted_iota(jnp.int32, (256, 256), 0) % 128
            lane = lax.broadcasted_iota(jnp.int32, (256, 256), 1)
            value = jnp.where((q >= 64) & (lane >= 192), other, value)
        for u in range(2):
            reals.append(value[:128, u * 128 : u * 128 + 128])
            imags.append(value[128:, u * 128 : u * 128 + 128])
        if t % 4 == 3:
            put(out_ref, t // 4, reals)
            put(out_ref, 2 + t // 4, imags)
            reals, imags = [], []


def columns(x_ref, far_ref, near_ref, tw_ref, table_ref, out_ref):
    long_ref, ilong_ref = table_ref.at[0:512, :], table_ref.at[512:1024, :]
    short_ref, ishort_ref = [
        jnp.concatenate([table_ref[k : k + 256, :], table_ref[k + 256 : k + 512, :]], axis=1)
        for k in (1024, 1536)
    ]
    cos, sin = tw_ref[:, :128], tw_ref[:, 128:]

    def some(blocks, extra):
        group = blocks[0] // 8
        real = jnp.concatenate(list(take(x_ref, group)), axis=1)
        imag = jnp.concatenate(list(take(x_ref, 2 + group)), axis=1)
        mid = table_times(long_ref, jnp.concatenate([real, imag], axis=0))
        joints = []
        for u in range(len(blocks)):
            real, imag = mid[:128, u * 128 : u * 128 + 128], mid[128:, u * 128 : u * 128 + 128]
            joints.append(jnp.concatenate([real * cos + imag * sin, imag * cos - real * sin], axis=1))
        spec = times_table(jnp.concatenate(joints, axis=0), short_ref)
        joints = []
        for u, b in enumerate(blocks):
            weight = far_ref[b] if b < FAR // 2 else near_ref[b - FAR // 2]
            joints.append(spec[u * 128 : u * 128 + 128] * jnp.concatenate([weight, weight], axis=1))
        if extra:
            weight = near_ref[16 - FAR // 2]
            u = len(blocks) - 1
            joints.append(spec[u * 128 : u * 128 + 128] * jnp.concatenate([weight, weight], axis=1))
        mixed = times_table(jnp.concatenate(joints, axis=0), ishort_ref)
        reals, imags = [], []
        for u in range(len(joints)):
            real, imag = mixed[u * 128 : u * 128 + 128, :128], mixed[u * 128 : u * 128 + 128, 128:]
            reals.append(real * cos - imag * sin)
            imags.append(imag * cos + real * sin)
        done = table_times(
            ilong_ref,
            jnp.concatenate([jnp.concatenate(reals, axis=1), jnp.concatenate(imags, axis=1)], axis=0),
        )
        last = len(joints) - 1
        put(out_ref, group, [done[:128, u * 128 : u * 128 + 128] for u in range(8)])
        put(out_ref, 2 + group, [done[128:, u * 128 : u * 128 + 128] for u in [*range(7), last]])

    some(range(8), False)
    some(range(8, 16), True)


def inverse_rows(x_ref, wide_ref, tw_ref, whole_ref, last_ref, out_ref, mid):

    def place(p, value):
        cos, sin = tw_ref[p : p + 1, :128], tw_ref[p : p + 1, 128:]
        real, imag = value[:, :128], value[:, 128:]
        mid[p * 64 : p * 64 + 64, :] = real * cos - imag * sin
        if p < 32:
            mid[(32 + p) * 64 : (33 + p) * 64, :] = imag * cos + real * sin

    for t in range(8):
        if t % 4 == 0:
            reals, imags = take(x_ref, t // 4), take(x_ref, 2 + t // 4)
        u = t % 4 * 2
        real = jnp.concatenate([reals[u], reals[u + 1]], axis=1)
        imag = jnp.concatenate([imags[u], imags[u + 1]], axis=1)
        joint = jnp.concatenate([real, imag], axis=0).T
        if t == 7:
            slot = lax.broadcasted_iota(jnp.int32, (256, 256), 0)
            q = lax.broadcasted_iota(jnp.int32, (256, 256), 1) % 128
            mid[0:64, :] = times_table(joint[192:, :], last_ref)
            joint = jnp.where((slot >= 192) & (q >= 64), 0.0, joint)
        result = times_table(joint, whole_ref)
        for k in range(4):
            place(4 * t + k + 1, result[k * 64 : k * 64 + 64, :])

    def groups(step, carry):
        base = pl.multiple_of(step * 16, 16)
        left = [mid[pl.ds(pp * 64 + base, 8), :] for pp in range(64)]
        right = [mid[pl.ds(pp * 64 + base + 8, 8), :] for pp in range(64)]
        block = jnp.concatenate([jnp.concatenate(left, axis=0), jnp.concatenate(right, axis=0)], axis=1)
        field = table_times(wide_ref, block)
        for c in range(8):
            for h in range(8):
                row = (c * 8 + h) * 8
                for g in range(2):
                    out_ref[c, pl.ds(base + g * 8, 8), h * 128 : h * 128 + 128] = field[
                        row : row + 8, g * 128 : g * 128 + 128
                    ]
        return carry

    lax.fori_loop(0, 4, groups, 0)


def tile_sums(slot_ref, field_ref, prev_ref, sums_ref, cells):
    for block in range(8):
        for h in range(8):
            lanes = slice(h * 128, h * 128 + 128)
            state = persist * prev_ref[block, :, lanes] + innovate * field_ref[block, :, lanes]
            rain = jnp.exp(log_mean + log_scale * state)
            cells[h, block : block + 1, :] = jnp.sum(rain, axis=0, keepdims=True)
    dest = lax.broadcasted_iota(jnp.int32, (DEV, 128), 0) * CAP
    lane = lax.broadcasted_iota(jnp.int32, (DEV, 128), 1)
    place = jnp.where(lane < CAP, dest + lane, -1)
    total = jnp.zeros((DEV, 128), F32)
    for h in range(8):
        half = jnp.sum(cells[h], axis=1, keepdims=True)
        for a in range(4):
            tile = (half[2 * a : 2 * a + 1] + half[2 * a + 1 : 2 * a + 2]) * (1.0 / (TILE * TILE))
            total = total + jnp.where(place == slot_ref[a * 8 + h], tile, 0.0)
    sums_ref[...] = total


def next_state(field_ref, prev_ref, state_ref):
    state_ref[...] = persist * prev_ref[...] + innovate * field_ref[...]


def reversal():
    flip = np.zeros((128, 128), np.float32)
    for k in range(1, 128):
        flip[k, 128 - k] = 1.0
    first = np.zeros((128, 128), np.float32)
    first[0, 0] = 1.0
    return np.concatenate([np.eye(128, dtype=np.float32), flip, first], axis=1).astype(ml_dtypes.bfloat16)


def exact_parts(rows):
    a = rows.astype(BF)
    rest = rows - a.astype(F32)
    b = rest.astype(BF)
    return a, b, (rest - b.astype(F32)).astype(BF)


def unfold(ref, group, backward):
    order = range(63, -1, -1) if backward else range(64)
    rows = slice(group * 8, group * 8 + 8)
    return jnp.swapaxes(jnp.stack([ref[rows, k * 128 : k * 128 + 128] for k in order]), 0, 1)


def weight_block(own, rev, flip_ref, d, p):
    rows = [
        jnp.concatenate([a, b, pltpu.roll(b, 1, 0)], axis=1) for a, b in zip(own, rev, strict=True)
    ]
    joint = jnp.concatenate(rows, axis=0)
    dims = ((1,), (1,))
    both = sum(dot(flip_ref[...], part, dims) for part in exact_parts(joint))
    shape = (128, len(own) * 64)
    ka = lax.broadcasted_iota(jnp.int32, shape, 0)
    lane = lax.broadcasted_iota(jnp.int32, shape, 1)
    k0 = ka + 128 * (lane % 64)
    f0 = jnp.where(k0 < N // 2, k0, k0 - N).astype(F32)
    k1 = d * 64 + p(lane // 64)
    f1 = jnp.where(k1 < N // 2, k1, k1 - N).astype(F32)
    width_sq = float((N // 128) * (N // 128))
    envelope = 1.0 + bump_height / (1.0 + (f0 * f0 + f1 * f1) / width_sq)
    return both * (envelope * (0.5 / (N * N)))


def put_weight(out_ref, first, value):
    for b in range(value.shape[1] // 128):
        out_ref[first + b] = value[:, b * 128 : b * 128 + 128]


def far_weights(d_ref, amp_ref, far_ref, flip_ref, out_ref):
    d = d_ref[0]
    own = [row for g in range(FAR // 8 + 1) for row in unfold(amp_ref, g, False)]
    rev = [row for g in range(FAR // 8) for row in unfold(far_ref, g, True)]
    for s in range(0, FAR, 8):
        mirrored = [rev[FAR - 1 - k] for k in range(s, s + 8)]
        value = weight_block(own[s + 1 : s + 9], mirrored, flip_ref, d, lambda k, s=s: k + (s + 1))
        put_weight(out_ref, s // 2, value)


def near_weights(d_ref, amp_ref, near_ref, row_ref, flip_ref, out_ref):
    d = d_ref[0]
    low = d < 64
    middle = d == 64
    own = [row for g in range(5) for row in unfold(amp_ref, g, False)]
    rev = [row for g in range(4 - FAR // 8) for row in unfold(near_ref, g, True)]
    row = row_ref[...]
    turn = lax.broadcasted_iota(jnp.int32, (64, 64), 0) + lax.broadcasted_iota(jnp.int32, (64, 64), 1) == 63
    turned = sum(dot(turn.astype(BF), part) for part in exact_parts(row))
    back = unfold(amp_ref, 0, True)[0]
    own_tail = jnp.where(low, own[32], own[0])
    rev_tail = jnp.where(low, rev[0], jnp.where(middle, back, turned))
    own_all = own[1:32] + [own_tail]
    rev_all = [None] * FAR + [rev[31 - k] for k in range(FAR, 31)] + [rev_tail]

    def plain(k, s):
        return jnp.where(k + s < 31, k + (s + 1), jnp.where(low, 32, 0))

    for s in range(FAR, 32, 8):
        value = weight_block(own_all[s : s + 8], rev_all[s : s + 8], flip_ref, d, lambda k, s=s: plain(k, s))
        put_weight(out_ref, (s - FAR) // 2, value)
    value = weight_block(
        [own[31], jnp.where(middle, row, own_tail)],
        [rev[1], jnp.where(middle, turned, rev_tail)],
        flip_ref,
        d,
        lambda k: jnp.where(k == 0, 31, jnp.where(low, 32, jnp.where(middle, -64 * 64, 0))),
    )
    put_weight(out_ref, 16 - FAR // 2, value)


def catchment_rows(catch_id, owner_map, devices):
    owners = owner_map[:, 0]
    hits = (owners[:, None] == jnp.arange(devices, dtype=jnp.int32)[None, :]).astype(jnp.int32)
    ranks = jnp.sum(hits * (jnp.cumsum(hits, axis=0) - 1), axis=1)
    slot = owners * CAP + ranks
    matches = catch_id.reshape(-1)[:, None] == jnp.arange(owners.shape[0], dtype=jnp.int32)[None, :]
    return jnp.sum(jnp.where(matches, slot[None, :], 0), axis=1)


def shards(white_noise, amplitude, state_prev, catch_id, owner_map, unit_graph, queue_prev):
    d = lax.axis_index(BOTH)
    flat = jax.ShapeDtypeStruct((DEV, 32, 128), F32)
    slab = lax.all_to_all(white_noise.reshape(8, 64, 1024), "col", 0, 0, tiled=True)
    small = np.stack([real_forward(), real_inverse()])
    near = lax.ppermute(amplitude[32 : 64 - FAR], BOTH, [(i, DEV - 1 - i) for i in range(DEV)])
    far = lax.ppermute(amplitude[64 - FAR : 64], "row", [(i, 15 - i) for i in range(16)])
    partner = lax.ppermute(
        amplitude[0:1], BOTH, [(0, 64)] + [(i, DEV - i) for i in range(1, 64)]
    )
    forward_wide, inverse_wide = call(
        widen, [jax.ShapeDtypeStruct((1024, 512), BF)] * 2, flops=100_000_000, bytes_accessed=2_000_000
    )(small)
    tile_slot = catchment_rows(catch_id, owner_map, DEV).astype(jnp.int32)
    device = d.astype(jnp.int32).reshape(1)
    scalar, vector = pl.BlockSpec(memory_space=pltpu.SMEM), pl.BlockSpec(memory_space=pltpu.VMEM)

    def weigh(body, blocks, *args):
        return pl.pallas_call(
            body,
            out_shape=jax.ShapeDtypeStruct((blocks, 128, 128), F32),
            in_specs=[scalar] + [vector] * len(args),
            compiler_params=pltpu.CompilerParams(vmem_limit_bytes=24 << 20),
            cost_estimate=pl.CostEstimate(flops=300_000_000, bytes_accessed=3_000_000, transcendentals=0),
        )(device, *args)

    flip = reversal()
    near_weight = weigh(near_weights, 17 - FAR // 2, amplitude, near, partner.reshape(64, 128), flip)
    slab, near_weight, far, tile_slot, forward_wide, inverse_wide = lax.optimization_barrier(
        (slab, near_weight, far, tile_slot, forward_wide, inverse_wide)
    )
    far = lax.ppermute(far, "col", [(i, 7 - i) for i in range(8)])
    far_weight = weigh(far_weights, FAR // 2, amplitude, far, flip)

    tw_row = row_twiddle()
    whole, forward_last, inverse_last = row_tables()
    spec = pl.pallas_call(
        forward_rows,
        out_shape=flat,
        in_specs=[pl.BlockSpec(memory_space=pl.ANY)] * 2 + [vector] * 3,
        scratch_shapes=[
            pltpu.VMEM((33 * 64, 256), F32),
            pltpu.VMEM((8, 64, 1024), F32),
            pltpu.VMEM((1024, 512), BF),
            pltpu.SemaphoreType.DMA((5,)),
        ],
        compiler_params=pltpu.CompilerParams(vmem_limit_bytes=24 << 20),
        cost_estimate=pl.CostEstimate(flops=2_000_000_000, bytes_accessed=6_000_000, transcendentals=0),
    )(slab, forward_wide, tw_row, stacked(whole), stacked(forward_last))
    spec, far_weight = lax.optimization_barrier((spec, far_weight))
    spec = lax.all_to_all(spec, BOTH, 0, 0, tiled=True)
    long, short = col_tables(-1.0)
    ilong, ishort = col_tables(1.0)
    tables = np.concatenate([stacked(table) for table in (long, ilong, short, ishort)], axis=0)
    shaped = call(columns, flat)(spec, far_weight, near_weight, col_twiddle(), tables)
    shaped = lax.all_to_all(shaped, BOTH, 0, 0, tiled=True)
    slab_type = jax.ShapeDtypeStruct((8, 64, 1024), F32)
    field = call(inverse_rows, slab_type, [pltpu.VMEM((64 * 64, 128), F32)])(
        shaped, inverse_wide, tw_row, whole, inverse_last
    )
    filtered = lax.all_to_all(field, "col", 0, 0, tiled=True)
    prev = state_prev.reshape(8, 64, 1024)
    sums = pl.pallas_call(
        tile_sums,
        out_shape=jax.ShapeDtypeStruct((DEV, 128), F32),
        in_specs=[scalar] + [vector] * 2,
        scratch_shapes=[pltpu.VMEM((8, 8, 128), F32)],
        compiler_params=pltpu.CompilerParams(vmem_limit_bytes=24 << 20),
        cost_estimate=pl.CostEstimate(flops=5_000_000, bytes_accessed=4_000_000, transcendentals=500_000),
    )(tile_slot, filtered, prev)
    state_new = call(next_state, slab_type, flops=2_000_000)(filtered, prev)
    received = lax.all_to_all(sums.reshape(DEV, 1, 128), BOTH, 0, 0, tiled=True)
    slot_rain = received.sum(axis=(0, 1))[:CAP]
    shifted = jnp.concatenate(
        [queue_prev[1:], jnp.zeros((1, queue_prev.shape[1]), jnp.float32)], axis=0
    )
    flow_queue = shifted + unit_graph * slot_rain[None, :]
    return (state_new.reshape(512, 1024), flow_queue)


def solution(mesh):
    return jax.shard_map(
        shards,
        mesh=mesh,
        in_specs=(
            P("row", "col"),
            P(BOTH, None),
            P("row", "col"),
            P("row", "col"),
            P(),
            P(None, BOTH),
            P(None, BOTH),
        ),
        out_specs=(P("row", "col"), P(None, BOTH)),
        check_vma=False,
    )
```

```python
from functools import partial

import jax
import jax.numpy as jnp
import ml_dtypes
import numpy as np
from jax import lax
from jax.experimental import pallas as pl
from jax.experimental.pallas import tpu as pltpu
from jax.sharding import PartitionSpec as P

TILE = 128
CAP = 32
N = 8192
DEV = 128
FAR = 8
BOTH = ("row", "col")

bump_height = 64.0
persist = 0.8
innovate = 0.6
log_mean = -0.3
log_scale = 0.6

BF = jnp.bfloat16
F32 = jnp.float32


def hi_lo(table):
    table = np.asarray(table, np.float64)
    hi = table.astype(ml_dtypes.bfloat16)
    lo = (table - hi.astype(np.float64)).astype(ml_dtypes.bfloat16)
    return np.concatenate([hi, lo], axis=1)


def stacked(table):
    half = table.shape[1] // 2
    return np.concatenate([table[:, :half], table[:, half:]], axis=0)


def angle(left, right, length):
    return 2.0 * np.pi / length * (np.outer(left, right) % length)


def real_forward():
    turn = angle(np.arange(64), np.arange(64), 64)
    table = np.concatenate([np.cos(turn[:33]), -np.sin(turn[1:32])], axis=0)
    return hi_lo(table)


def real_inverse():
    turn = angle(np.arange(64), np.arange(64), 64)
    real = 2.0 * np.cos(turn[:, :33])
    real[:, 0] = 1.0
    table = np.concatenate([real, -2.0 * np.sin(turn[:, 1:32])], axis=1)
    return hi_lo(table)


def widen(small_ref, fwd_ref, inv_ref):
    tall = (
        lax.broadcasted_iota(jnp.int32, (512, 64), 0) // 8 == lax.broadcasted_iota(jnp.int32, (512, 64), 1)
    ).astype(BF)
    row = lax.broadcasted_iota(jnp.int32, (512, 512), 0)
    col = lax.broadcasted_iota(jnp.int32, (512, 512), 1)
    same = row % 8 == col % 8
    for k, ref in enumerate([fwd_ref, inv_ref]):
        for half in range(2):
            small = small_ref[k, :, half * 64 : half * 64 + 64]
            grown = dot(dot(tall, small).astype(BF), tall, ((1,), (1,)))
            ref[half * 512 : half * 512 + 512, :] = jnp.where(same, grown, 0.0).astype(BF)


def row_twiddle():
    turn = angle(np.arange(33), np.arange(128), N)
    return np.concatenate([np.cos(turn), np.sin(turn)], axis=1).astype(np.float32)


def row_tables():
    turn = angle(np.arange(128), np.arange(128), 128)
    cos, sin = np.cos(turn), np.sin(turn)
    high = (np.arange(128) >= 64).astype(np.float64)[:, None]
    imag = -sin * high
    imag[64] = 1.0
    forward = np.concatenate([cos * high, imag], axis=0)
    top, bottom = 2.0 * cos * high, -2.0 * sin * high
    top[64] = cos[64]
    bottom[64] = 1.0
    inverse = np.concatenate([top, bottom], axis=0)
    return hi_lo(np.block([[cos, sin], [-sin, cos]])), hi_lo(forward), hi_lo(inverse)


def col_tables(sign):
    turn = angle(np.arange(128), np.arange(128), 128)
    cos, sin = np.cos(turn), sign * np.sin(turn)
    long = np.block([[cos, -sin], [sin, cos]])
    turn = angle(np.arange(64), np.arange(64), 64)
    cos, sin = np.kron(np.eye(2), np.cos(turn)), np.kron(np.eye(2), sign * np.sin(turn))
    short = np.block([[cos, sin], [-sin, cos]])
    return hi_lo(long), hi_lo(short)


def col_twiddle():
    turn = angle(np.arange(128), np.arange(128) % 64, N)
    return np.concatenate([np.cos(turn), np.sin(turn)], axis=1).astype(np.float32)


def split(value):
    hi = value.astype(BF)
    return hi, (value - hi.astype(F32)).astype(BF)


def dot(left, right, dims=((1,), (0,))):
    return lax.dot_general(left, right, (dims, ((), ())), preferred_element_type=F32)


def times_table(value, table):
    rows, half = value.shape[0], table.shape[1] // 2
    hi, lo = split(value)
    first = dot(jnp.concatenate([hi, lo], axis=0), table[:, :half])
    return first[:rows] + first[rows:] + dot(hi, table[:, half:])


def table_times(table, value, dims=((1,), (0,))):
    rows = table.shape[0] // 2
    hi, lo = split(value)
    first = dot(table[...], hi, dims)
    return first[:rows] + first[rows:] + dot(table[:rows, :], lo, dims)


def take(ref, group):
    return jnp.swapaxes(ref[:, group * 8 : group * 8 + 8, :], 0, 1)


def put(ref, group, blocks):
    ref[:, group * 8 : group * 8 + 8, :] = jnp.swapaxes(jnp.stack(blocks), 0, 1)


def call(body, out, scratch=(), limit=24, flops=2_000_000_000, bytes_accessed=6_000_000):
    return pl.pallas_call(
        body,
        out_shape=out,
        scratch_shapes=list(scratch),
        compiler_params=pltpu.CompilerParams(vmem_limit_bytes=limit << 20),
        cost_estimate=pl.CostEstimate(flops=flops, bytes_accessed=bytes_accessed, transcendentals=0),
    )


def forward_rows(x_hbm, wide_hbm, tw_ref, whole_ref, last_ref, out_ref, mid, x_ref, wide_ref, sems):
    def fetch(step):
        rows = pl.ds(pl.multiple_of(step * 16, 16), 16)
        return pltpu.make_async_copy(x_hbm.at[:, rows, :], x_ref.at[:, rows, :], sems.at[step])

    table = pltpu.make_async_copy(wide_hbm, wide_ref, sems.at[4])
    table.start()
    for step in range(4):
        fetch(step).start()
    table.wait()

    def groups(step, carry):
        base = pl.multiple_of(step * 16, 16)
        fetch(step).wait()
        left = [x_ref[c, pl.ds(base, 8), h * 128 : h * 128 + 128] for c in range(8) for h in range(8)]
        right = [x_ref[c, pl.ds(base + 8, 8), h * 128 : h * 128 + 128] for c in range(8) for h in range(8)]
        block = jnp.concatenate([jnp.concatenate(left, axis=0), jnp.concatenate(right, axis=0)], axis=1)
        spec = table_times(wide_ref, block)
        for p in range(33):
            cos, sin = tw_ref[p : p + 1, :128], tw_ref[p : p + 1, 128:]
            for g in range(2):
                lanes = slice(g * 128, g * 128 + 128)
                rows = pl.ds(p * 64 + base + g * 8, 8)
                real = spec[p * 8 : p * 8 + 8, lanes]
                if p == 0:
                    mid[rows, :128] = real
                    continue
                if p == 32:
                    mid[rows, :128] = real * cos
                    mid[rows, 128:] = -(real * sin)
                    continue
                imag = spec[(32 + p) * 8 : (32 + p) * 8 + 8, lanes]
                mid[rows, :128] = real * cos + imag * sin
                mid[rows, 128:] = imag * cos - real * sin
        return carry

    lax.fori_loop(0, 4, groups, 0)

    reals, imags = [], []
    for t in range(8):
        rows = mid[(4 * t + 1) * 64 : (4 * t + 5) * 64, :]
        value = table_times(whole_ref, rows, ((1,), (1,)))
        if t == 7:
            rows = jnp.concatenate([jnp.zeros((192, 128), F32), mid[0:64, :128]], axis=0)
            other = table_times(last_ref, rows, ((1,), (1,)))
            q = lax.broadcasted_iota(jnp.int32, (256, 256), 0) % 128
            lane = lax.broadcasted_iota(jnp.int32, (256, 256), 1)
            value = jnp.where((q >= 64) & (lane >= 192), other, value)
        for u in range(2):
            reals.append(value[:128, u * 128 : u * 128 + 128])
            imags.append(value[128:, u * 128 : u * 128 + 128])
        if t % 4 == 3:
            put(out_ref, t // 4, reals)
            put(out_ref, 2 + t // 4, imags)
            reals, imags = [], []


def columns(x_ref, far_ref, near_ref, tw_ref, table_ref, out_ref):
    long_ref, ilong_ref = table_ref.at[0:512, :], table_ref.at[512:1024, :]
    short_ref, ishort_ref = [
        jnp.concatenate([table_ref[k : k + 256, :], table_ref[k + 256 : k + 512, :]], axis=1)
        for k in (1024, 1536)
    ]
    cos, sin = tw_ref[:, :128], tw_ref[:, 128:]

    def some(blocks, extra):
        group = blocks[0] // 8
        real = jnp.concatenate(list(take(x_ref, group)), axis=1)
        imag = jnp.concatenate(list(take(x_ref, 2 + group)), axis=1)
        mid = table_times(long_ref, jnp.concatenate([real, imag], axis=0))
        joints = []
        for u in range(len(blocks)):
            real, imag = mid[:128, u * 128 : u * 128 + 128], mid[128:, u * 128 : u * 128 + 128]
            joints.append(jnp.concatenate([real * cos + imag * sin, imag * cos - real * sin], axis=1))
        spec = times_table(jnp.concatenate(joints, axis=0), short_ref)
        joints = []
        for u, b in enumerate(blocks):
            weight = far_ref[b] if b < FAR // 2 else near_ref[b - FAR // 2]
            joints.append(spec[u * 128 : u * 128 + 128] * jnp.concatenate([weight, weight], axis=1))
        if extra:
            weight = near_ref[16 - FAR // 2]
            u = len(blocks) - 1
            joints.append(spec[u * 128 : u * 128 + 128] * jnp.concatenate([weight, weight], axis=1))
        mixed = times_table(jnp.concatenate(joints, axis=0), ishort_ref)
        reals, imags = [], []
        for u in range(len(joints)):
            real, imag = mixed[u * 128 : u * 128 + 128, :128], mixed[u * 128 : u * 128 + 128, 128:]
            reals.append(real * cos - imag * sin)
            imags.append(imag * cos + real * sin)
        done = table_times(
            ilong_ref,
            jnp.concatenate([jnp.concatenate(reals, axis=1), jnp.concatenate(imags, axis=1)], axis=0),
        )
        last = len(joints) - 1
        put(out_ref, group, [done[:128, u * 128 : u * 128 + 128] for u in range(8)])
        put(out_ref, 2 + group, [done[128:, u * 128 : u * 128 + 128] for u in [*range(7), last]])

    some(range(8), False)
    some(range(8, 16), True)


def inverse_rows(x_ref, wide_ref, tw_ref, whole_ref, last_ref, out_ref, mid):

    def place(p, value):
        cos, sin = tw_ref[p : p + 1, :128], tw_ref[p : p + 1, 128:]
        real, imag = value[:, :128], value[:, 128:]
        mid[p * 64 : p * 64 + 64, :] = real * cos - imag * sin
        if p < 32:
            mid[(32 + p) * 64 : (33 + p) * 64, :] = imag * cos + real * sin

    for t in range(8):
        if t % 4 == 0:
            reals, imags = take(x_ref, t // 4), take(x_ref, 2 + t // 4)
        u = t % 4 * 2
        real = jnp.concatenate([reals[u], reals[u + 1]], axis=1)
        imag = jnp.concatenate([imags[u], imags[u + 1]], axis=1)
        joint = jnp.concatenate([real, imag], axis=0).T
        if t == 7:
            slot = lax.broadcasted_iota(jnp.int32, (256, 256), 0)
            q = lax.broadcasted_iota(jnp.int32, (256, 256), 1) % 128
            mid[0:64, :] = times_table(joint[192:, :], last_ref)
            joint = jnp.where((slot >= 192) & (q >= 64), 0.0, joint)
        result = times_table(joint, whole_ref)
        for k in range(4):
            place(4 * t + k + 1, result[k * 64 : k * 64 + 64, :])

    def groups(step, carry):
        base = pl.multiple_of(step * 16, 16)
        left = [mid[pl.ds(pp * 64 + base, 8), :] for pp in range(64)]
        right = [mid[pl.ds(pp * 64 + base + 8, 8), :] for pp in range(64)]
        block = jnp.concatenate([jnp.concatenate(left, axis=0), jnp.concatenate(right, axis=0)], axis=1)
        field = table_times(wide_ref, block)
        for c in range(8):
            for h in range(8):
                row = (c * 8 + h) * 8
                for g in range(2):
                    out_ref[c, pl.ds(base + g * 8, 8), h * 128 : h * 128 + 128] = field[
                        row : row + 8, g * 128 : g * 128 + 128
                    ]
        return carry

    lax.fori_loop(0, 4, groups, 0)


def tile_sums(slot_ref, field_ref, prev_ref, sums_ref, cells):
    for block in range(8):
        for h in range(8):
            lanes = slice(h * 128, h * 128 + 128)
            state = persist * prev_ref[block, :, lanes] + innovate * field_ref[block, :, lanes]
            rain = jnp.exp(log_mean + log_scale * state)
            cells[h, block : block + 1, :] = jnp.sum(rain, axis=0, keepdims=True)
    dest = lax.broadcasted_iota(jnp.int32, (DEV, 128), 0) * CAP
    lane = lax.broadcasted_iota(jnp.int32, (DEV, 128), 1)
    place = jnp.where(lane < CAP, dest + lane, -1)
    total = jnp.zeros((DEV, 128), F32)
    for h in range(8):
        half = jnp.sum(cells[h], axis=1, keepdims=True)
        for a in range(4):
            tile = (half[2 * a : 2 * a + 1] + half[2 * a + 1 : 2 * a + 2]) * (1.0 / (TILE * TILE))
            total = total + jnp.where(place == slot_ref[a * 8 + h], tile, 0.0)
    sums_ref[...] = total


def next_state(field_ref, prev_ref, state_ref):
    state_ref[...] = persist * prev_ref[...] + innovate * field_ref[...]


def reversal():
    flip = np.zeros((128, 128), np.float32)
    for k in range(1, 128):
        flip[k, 128 - k] = 1.0
    first = np.zeros((128, 128), np.float32)
    first[0, 0] = 1.0
    return np.concatenate([np.eye(128, dtype=np.float32), flip, first], axis=1).astype(ml_dtypes.bfloat16)


def exact_parts(rows):
    a = rows.astype(BF)
    rest = rows - a.astype(F32)
    b = rest.astype(BF)
    return a, b, (rest - b.astype(F32)).astype(BF)


def unfold(ref, group, backward):
    order = range(63, -1, -1) if backward else range(64)
    rows = slice(group * 8, group * 8 + 8)
    return jnp.swapaxes(jnp.stack([ref[rows, k * 128 : k * 128 + 128] for k in order]), 0, 1)


def weight_block(own, rev, flip_ref, d, p):
    rows = [
        jnp.concatenate([a, b, pltpu.roll(b, 1, 0)], axis=1) for a, b in zip(own, rev, strict=True)
    ]
    joint = jnp.concatenate(rows, axis=0)
    dims = ((1,), (1,))
    both = sum(dot(flip_ref[...], part, dims) for part in exact_parts(joint))
    shape = (128, len(own) * 64)
    ka = lax.broadcasted_iota(jnp.int32, shape, 0)
    lane = lax.broadcasted_iota(jnp.int32, shape, 1)
    k0 = ka + 128 * (lane % 64)
    f0 = jnp.where(k0 < N // 2, k0, k0 - N).astype(F32)
    k1 = d * 64 + p(lane // 64)
    f1 = jnp.where(k1 < N // 2, k1, k1 - N).astype(F32)
    width_sq = float((N // 128) * (N // 128))
    envelope = 1.0 + bump_height / (1.0 + (f0 * f0 + f1 * f1) / width_sq)
    return both * (envelope * (0.5 / (N * N)))


def put_weight(out_ref, first, value):
    for b in range(value.shape[1] // 128):
        out_ref[first + b] = value[:, b * 128 : b * 128 + 128]


def far_weights(d_ref, amp_ref, far_ref, flip_ref, out_ref):
    d = d_ref[0]
    own = [row for g in range(FAR // 8 + 1) for row in unfold(amp_ref, g, False)]
    rev = [row for g in range(FAR // 8) for row in unfold(far_ref, g, True)]
    for s in range(0, FAR, 8):
        mirrored = [rev[FAR - 1 - k] for k in range(s, s + 8)]
        value = weight_block(own[s + 1 : s + 9], mirrored, flip_ref, d, lambda k, s=s: k + (s + 1))
        put_weight(out_ref, s // 2, value)


def near_weights(d_ref, amp_ref, near_ref, row_ref, flip_ref, out_ref):
    d = d_ref[0]
    low = d < 64
    middle = d == 64
    own = [row for g in range(5) for row in unfold(amp_ref, g, False)]
    rev = [row for g in range(4 - FAR // 8) for row in unfold(near_ref, g, True)]
    row = row_ref[...]
    turn = lax.broadcasted_iota(jnp.int32, (64, 64), 0) + lax.broadcasted_iota(jnp.int32, (64, 64), 1) == 63
    turned = sum(dot(turn.astype(BF), part) for part in exact_parts(row))
    back = unfold(amp_ref, 0, True)[0]
    own_tail = jnp.where(low, own[32], own[0])
    rev_tail = jnp.where(low, rev[0], jnp.where(middle, back, turned))
    own_all = own[1:32] + [own_tail]
    rev_all = [None] * FAR + [rev[31 - k] for k in range(FAR, 31)] + [rev_tail]

    def plain(k, s):
        return jnp.where(k + s < 31, k + (s + 1), jnp.where(low, 32, 0))

    for s in range(FAR, 32, 8):
        value = weight_block(own_all[s : s + 8], rev_all[s : s + 8], flip_ref, d, lambda k, s=s: plain(k, s))
        put_weight(out_ref, (s - FAR) // 2, value)
    value = weight_block(
        [own[31], jnp.where(middle, row, own_tail)],
        [rev[1], jnp.where(middle, turned, rev_tail)],
        flip_ref,
        d,
        lambda k: jnp.where(k == 0, 31, jnp.where(low, 32, jnp.where(middle, -64 * 64, 0))),
    )
    put_weight(out_ref, 16 - FAR // 2, value)


def catchment_rows(catch_id, owner_map, devices):
    owners = owner_map[:, 0]
    hits = (owners[:, None] == jnp.arange(devices, dtype=jnp.int32)[None, :]).astype(jnp.int32)
    ranks = jnp.sum(hits * (jnp.cumsum(hits, axis=0) - 1), axis=1)
    slot = owners * CAP + ranks
    matches = catch_id.reshape(-1)[:, None] == jnp.arange(owners.shape[0], dtype=jnp.int32)[None, :]
    return jnp.sum(jnp.where(matches, slot[None, :], 0), axis=1)


def shards(white_noise, amplitude, state_prev, catch_id, owner_map, unit_graph, queue_prev):
    d = lax.axis_index(BOTH)
    flat = jax.ShapeDtypeStruct((DEV, 32, 128), F32)
    slab = lax.all_to_all(white_noise.reshape(8, 64, 1024), "col", 0, 0, tiled=True)
    small = np.stack([real_forward(), real_inverse()])
    near = lax.ppermute(amplitude[32 : 64 - FAR], BOTH, [(i, DEV - 1 - i) for i in range(DEV)])
    far = lax.ppermute(amplitude[64 - FAR : 64], "row", [(i, 15 - i) for i in range(16)])
    partner = lax.ppermute(
        amplitude[0:1], BOTH, [(0, 64)] + [(i, DEV - i) for i in range(1, 64)]
    )
    forward_wide, inverse_wide = call(
        widen, [jax.ShapeDtypeStruct((1024, 512), BF)] * 2, flops=100_000_000, bytes_accessed=2_000_000
    )(small)
    tile_slot = catchment_rows(catch_id, owner_map, DEV).astype(jnp.int32)
    device = d.astype(jnp.int32).reshape(1)
    scalar, vector = pl.BlockSpec(memory_space=pltpu.SMEM), pl.BlockSpec(memory_space=pltpu.VMEM)

    def weigh(body, device, blocks, *args):
        return pl.pallas_call(
            body,
            out_shape=jax.ShapeDtypeStruct((blocks, 128, 128), F32),
            in_specs=[scalar] + [vector] * len(args),
            compiler_params=pltpu.CompilerParams(vmem_limit_bytes=24 << 20),
            cost_estimate=pl.CostEstimate(flops=300_000_000, bytes_accessed=3_000_000, transcendentals=0),
        )(device, *args)

    flip = reversal()
    near, far, partner, tile_slot, forward_wide, inverse_wide = lax.optimization_barrier(
        (near, far, partner, tile_slot, forward_wide, inverse_wide)
    )
    near_weight = weigh(near_weights, device, 17 - FAR // 2, amplitude, near, partner.reshape(64, 128), flip)
    far = lax.ppermute(far, "col", [(i, 7 - i) for i in range(8)])
    slab, near_weight = lax.optimization_barrier((slab, near_weight))
    tw_row = row_twiddle()
    whole, forward_last, inverse_last = row_tables()
    spec = pl.pallas_call(
        forward_rows,
        out_shape=flat,
        in_specs=[pl.BlockSpec(memory_space=pltpu.MemorySpace.HBM)] * 2 + [vector] * 3,
        scratch_shapes=[
            pltpu.VMEM((33 * 64, 256), F32),
            pltpu.VMEM((8, 64, 1024), F32),
            pltpu.VMEM((1024, 512), BF),
            pltpu.SemaphoreType.DMA((5,)),
        ],
        compiler_params=pltpu.CompilerParams(vmem_limit_bytes=24 << 20),
        cost_estimate=pl.CostEstimate(flops=2_000_000_000, bytes_accessed=6_000_000, transcendentals=0),
    )(slab, forward_wide, tw_row, stacked(whole), stacked(forward_last))
    spec, device = lax.optimization_barrier((spec, device))
    far_weight = weigh(far_weights, device, FAR // 2, amplitude, far, flip)
    spec, far_weight = lax.optimization_barrier((spec, far_weight))
    spec = lax.all_to_all(spec, BOTH, 0, 0, tiled=True)
    long, short = col_tables(-1.0)
    ilong, ishort = col_tables(1.0)
    tables = np.concatenate([stacked(table) for table in (long, ilong, short, ishort)], axis=0)
    shaped = call(columns, flat)(spec, far_weight, near_weight, col_twiddle(), tables)
    shaped = lax.all_to_all(shaped, BOTH, 0, 0, tiled=True)
    slab_type = jax.ShapeDtypeStruct((8, 64, 1024), F32)
    field = call(inverse_rows, slab_type, [pltpu.VMEM((64 * 64, 128), F32)])(
        shaped, inverse_wide, tw_row, whole, inverse_last
    )
    filtered = lax.all_to_all(field, "col", 0, 0, tiled=True)
    prev = state_prev.reshape(8, 64, 1024)
    sums = pl.pallas_call(
        tile_sums,
        out_shape=jax.ShapeDtypeStruct((DEV, 128), F32),
        in_specs=[scalar] + [vector] * 2,
        scratch_shapes=[pltpu.VMEM((8, 8, 128), F32)],
        compiler_params=pltpu.CompilerParams(vmem_limit_bytes=24 << 20),
        cost_estimate=pl.CostEstimate(flops=5_000_000, bytes_accessed=4_000_000, transcendentals=500_000),
    )(tile_slot, filtered, prev)
    state_new = call(next_state, slab_type, flops=2_000_000)(filtered, prev)
    received = lax.all_to_all(sums.reshape(DEV, 1, 128), BOTH, 0, 0, tiled=True)
    slot_rain = received.sum(axis=(0, 1))[:CAP]
    shifted = jnp.concatenate(
        [queue_prev[1:], jnp.zeros((1, queue_prev.shape[1]), jnp.float32)], axis=0
    )
    flow_queue = shifted + unit_graph * slot_rain[None, :]
    return (state_new.reshape(512, 1024), flow_queue)


def solution(mesh):
    return jax.shard_map(
        shards,
        mesh=mesh,
        in_specs=(
            P("row", "col"),
            P(BOTH, None),
            P("row", "col"),
            P("row", "col"),
            P(),
            P(None, BOTH),
            P(None, BOTH),
        ),
        out_specs=(P("row", "col"), P(None, BOTH)),
        check_vma=False,
    )
```

```python
from functools import partial

import jax
import jax.numpy as jnp
import ml_dtypes
import numpy as np
from jax import lax
from jax.experimental import pallas as pl
from jax.experimental.pallas import tpu as pltpu
from jax.sharding import PartitionSpec as P

TILE = 128
CAP = 32
N = 8192
DEV = 128
FAR = 16
BOTH = ("row", "col")

bump_height = 64.0
persist = 0.8
innovate = 0.6
log_mean = -0.3
log_scale = 0.6

BF = jnp.bfloat16
F32 = jnp.float32


def hi_lo(table):
    table = np.asarray(table, np.float64)
    hi = table.astype(ml_dtypes.bfloat16)
    lo = (table - hi.astype(np.float64)).astype(ml_dtypes.bfloat16)
    return np.concatenate([hi, lo], axis=1)


def stacked(table):
    half = table.shape[1] // 2
    return np.concatenate([table[:, :half], table[:, half:]], axis=0)


def angle(left, right, length):
    return 2.0 * np.pi / length * (np.outer(left, right) % length)


def real_forward():
    turn = angle(np.arange(64), np.arange(64), 64)
    table = np.concatenate([np.cos(turn[:33]), -np.sin(turn[1:32])], axis=0)
    return hi_lo(table)


def real_inverse():
    turn = angle(np.arange(64), np.arange(64), 64)
    real = 2.0 * np.cos(turn[:, :33])
    real[:, 0] = 1.0
    table = np.concatenate([real, -2.0 * np.sin(turn[:, 1:32])], axis=1)
    return hi_lo(table)


def widen(small_ref, fwd_ref, inv_ref):
    tall = (
        lax.broadcasted_iota(jnp.int32, (512, 64), 0) // 8 == lax.broadcasted_iota(jnp.int32, (512, 64), 1)
    ).astype(BF)
    row = lax.broadcasted_iota(jnp.int32, (512, 512), 0)
    col = lax.broadcasted_iota(jnp.int32, (512, 512), 1)
    same = row % 8 == col % 8
    for k, ref in enumerate([fwd_ref, inv_ref]):
        for half in range(2):
            small = small_ref[k, :, half * 64 : half * 64 + 64]
            grown = dot(dot(tall, small).astype(BF), tall, ((1,), (1,)))
            ref[half * 512 : half * 512 + 512, :] = jnp.where(same, grown, 0.0).astype(BF)


def row_twiddle():
    turn = angle(np.arange(33), np.arange(128), N)
    return np.concatenate([np.cos(turn), np.sin(turn)], axis=1).astype(np.float32)


def row_tables():
    turn = angle(np.arange(128), np.arange(128), 128)
    cos, sin = np.cos(turn), np.sin(turn)
    high = (np.arange(128) >= 64).astype(np.float64)[:, None]
    imag = -sin * high
    imag[64] = 1.0
    forward = np.concatenate([cos * high, imag], axis=0)
    top, bottom = 2.0 * cos * high, -2.0 * sin * high
    top[64] = cos[64]
    bottom[64] = 1.0
    inverse = np.concatenate([top, bottom], axis=0)
    return hi_lo(np.block([[cos, sin], [-sin, cos]])), hi_lo(forward), hi_lo(inverse)


def col_tables(sign):
    turn = angle(np.arange(128), np.arange(128), 128)
    cos, sin = np.cos(turn), sign * np.sin(turn)
    long = np.block([[cos, -sin], [sin, cos]])
    turn = angle(np.arange(64), np.arange(64), 64)
    cos, sin = np.kron(np.eye(2), np.cos(turn)), np.kron(np.eye(2), sign * np.sin(turn))
    short = np.block([[cos, sin], [-sin, cos]])
    return hi_lo(long), hi_lo(short)


def col_twiddle():
    turn = angle(np.arange(128), np.arange(128) % 64, N)
    return np.concatenate([np.cos(turn), np.sin(turn)], axis=1).astype(np.float32)


def split(value):
    hi = value.astype(BF)
    return hi, (value - hi.astype(F32)).astype(BF)


def dot(left, right, dims=((1,), (0,))):
    return lax.dot_general(left, right, (dims, ((), ())), preferred_element_type=F32)


def times_table(value, table):
    rows, half = value.shape[0], table.shape[1] // 2
    hi, lo = split(value)
    first = dot(jnp.concatenate([hi, lo], axis=0), table[:, :half])
    return first[:rows] + first[rows:] + dot(hi, table[:, half:])


def table_times(table, value, dims=((1,), (0,))):
    rows = table.shape[0] // 2
    hi, lo = split(value)
    first = dot(table[...], hi, dims)
    return first[:rows] + first[rows:] + dot(table[:rows, :], lo, dims)


def take(ref, group):
    return jnp.swapaxes(ref[:, group * 8 : group * 8 + 8, :], 0, 1)


def put(ref, group, blocks):
    ref[:, group * 8 : group * 8 + 8, :] = jnp.swapaxes(jnp.stack(blocks), 0, 1)


def call(body, out, scratch=(), limit=24, flops=2_000_000_000, bytes_accessed=6_000_000):
    return pl.pallas_call(
        body,
        out_shape=out,
        scratch_shapes=list(scratch),
        compiler_params=pltpu.CompilerParams(vmem_limit_bytes=limit << 20),
        cost_estimate=pl.CostEstimate(flops=flops, bytes_accessed=bytes_accessed, transcendentals=0),
    )


def forward_rows(x_hbm, wide_hbm, tw_ref, whole_ref, last_ref, out_ref, mid, x_ref, wide_ref, sems):
    def fetch(step):
        rows = pl.ds(pl.multiple_of(step * 16, 16), 16)
        return pltpu.make_async_copy(x_hbm.at[:, rows, :], x_ref.at[:, rows, :], sems.at[step])

    table = pltpu.make_async_copy(wide_hbm, wide_ref, sems.at[4])
    table.start()
    for step in range(4):
        fetch(step).start()
    table.wait()

    def groups(step, carry):
        base = pl.multiple_of(step * 16, 16)
        fetch(step).wait()
        left = [x_ref[c, pl.ds(base, 8), h * 128 : h * 128 + 128] for c in range(8) for h in range(8)]
        right = [x_ref[c, pl.ds(base + 8, 8), h * 128 : h * 128 + 128] for c in range(8) for h in range(8)]
        block = jnp.concatenate([jnp.concatenate(left, axis=0), jnp.concatenate(right, axis=0)], axis=1)
        spec = table_times(wide_ref, block)
        for p in range(33):
            cos, sin = tw_ref[p : p + 1, :128], tw_ref[p : p + 1, 128:]
            for g in range(2):
                lanes = slice(g * 128, g * 128 + 128)
                rows = pl.ds(p * 64 + base + g * 8, 8)
                real = spec[p * 8 : p * 8 + 8, lanes]
                if p == 0:
                    mid[rows, :128] = real
                    continue
                if p == 32:
                    mid[rows, :128] = real * cos
                    mid[rows, 128:] = -(real * sin)
                    continue
                imag = spec[(32 + p) * 8 : (32 + p) * 8 + 8, lanes]
                mid[rows, :128] = real * cos + imag * sin
                mid[rows, 128:] = imag * cos - real * sin
        return carry

    lax.fori_loop(0, 4, groups, 0)

    reals, imags = [], []
    for t in range(8):
        rows = mid[(4 * t + 1) * 64 : (4 * t + 5) * 64, :]
        value = table_times(whole_ref, rows, ((1,), (1,)))
        if t == 7:
            rows = jnp.concatenate([jnp.zeros((192, 128), F32), mid[0:64, :128]], axis=0)
            other = table_times(last_ref, rows, ((1,), (1,)))
            q = lax.broadcasted_iota(jnp.int32, (256, 256), 0) % 128
            lane = lax.broadcasted_iota(jnp.int32, (256, 256), 1)
            value = jnp.where((q >= 64) & (lane >= 192), other, value)
        for u in range(2):
            reals.append(value[:128, u * 128 : u * 128 + 128])
            imags.append(value[128:, u * 128 : u * 128 + 128])
        if t % 4 == 3:
            put(out_ref, t // 4, reals)
            put(out_ref, 2 + t // 4, imags)
            reals, imags = [], []


def columns(x_ref, far_ref, near_ref, tw_ref, table_ref, out_ref):
    long_ref, ilong_ref = table_ref.at[0:512, :], table_ref.at[512:1024, :]
    short_ref, ishort_ref = [
        jnp.concatenate([table_ref[k : k + 256, :], table_ref[k + 256 : k + 512, :]], axis=1)
        for k in (1024, 1536)
    ]
    cos, sin = tw_ref[:, :128], tw_ref[:, 128:]

    def some(blocks, extra):
        group = blocks[0] // 8
        real = jnp.concatenate(list(take(x_ref, group)), axis=1)
        imag = jnp.concatenate(list(take(x_ref, 2 + group)), axis=1)
        mid = table_times(long_ref, jnp.concatenate([real, imag], axis=0))
        joints = []
        for u in range(len(blocks)):
            real, imag = mid[:128, u * 128 : u * 128 + 128], mid[128:, u * 128 : u * 128 + 128]
            joints.append(jnp.concatenate([real * cos + imag * sin, imag * cos - real * sin], axis=1))
        spec = times_table(jnp.concatenate(joints, axis=0), short_ref)
        joints = []
        for u, b in enumerate(blocks):
            weight = far_ref[b] if b < FAR // 2 else near_ref[b - FAR // 2]
            joints.append(spec[u * 128 : u * 128 + 128] * jnp.concatenate([weight, weight], axis=1))
        if extra:
            weight = near_ref[16 - FAR // 2]
            u = len(blocks) - 1
            joints.append(spec[u * 128 : u * 128 + 128] * jnp.concatenate([weight, weight], axis=1))
        mixed = times_table(jnp.concatenate(joints, axis=0), ishort_ref)
        reals, imags = [], []
        for u in range(len(joints)):
            real, imag = mixed[u * 128 : u * 128 + 128, :128], mixed[u * 128 : u * 128 + 128, 128:]
            reals.append(real * cos - imag * sin)
            imags.append(imag * cos + real * sin)
        done = table_times(
            ilong_ref,
            jnp.concatenate([jnp.concatenate(reals, axis=1), jnp.concatenate(imags, axis=1)], axis=0),
        )
        last = len(joints) - 1
        put(out_ref, group, [done[:128, u * 128 : u * 128 + 128] for u in range(8)])
        put(out_ref, 2 + group, [done[128:, u * 128 : u * 128 + 128] for u in [*range(7), last]])

    some(range(8), False)
    some(range(8, 16), True)


def inverse_rows(x_ref, wide_ref, tw_ref, whole_ref, last_ref, out_ref, mid):

    def place(p, value):
        cos, sin = tw_ref[p : p + 1, :128], tw_ref[p : p + 1, 128:]
        real, imag = value[:, :128], value[:, 128:]
        mid[p * 64 : p * 64 + 64, :] = real * cos - imag * sin
        if p < 32:
            mid[(32 + p) * 64 : (33 + p) * 64, :] = imag * cos + real * sin

    for t in range(8):
        if t % 4 == 0:
            reals, imags = take(x_ref, t // 4), take(x_ref, 2 + t // 4)
        u = t % 4 * 2
        real = jnp.concatenate([reals[u], reals[u + 1]], axis=1)
        imag = jnp.concatenate([imags[u], imags[u + 1]], axis=1)
        joint = jnp.concatenate([real, imag], axis=0).T
        if t == 7:
            slot = lax.broadcasted_iota(jnp.int32, (256, 256), 0)
            q = lax.broadcasted_iota(jnp.int32, (256, 256), 1) % 128
            mid[0:64, :] = times_table(joint[192:, :], last_ref)
            joint = jnp.where((slot >= 192) & (q >= 64), 0.0, joint)
        result = times_table(joint, whole_ref)
        for k in range(4):
            place(4 * t + k + 1, result[k * 64 : k * 64 + 64, :])

    def groups(step, carry):
        base = pl.multiple_of(step * 16, 16)
        left = [mid[pl.ds(pp * 64 + base, 8), :] for pp in range(64)]
        right = [mid[pl.ds(pp * 64 + base + 8, 8), :] for pp in range(64)]
        block = jnp.concatenate([jnp.concatenate(left, axis=0), jnp.concatenate(right, axis=0)], axis=1)
        field = table_times(wide_ref, block)
        for c in range(8):
            for h in range(8):
                row = (c * 8 + h) * 8
                for g in range(2):
                    out_ref[c, pl.ds(base + g * 8, 8), h * 128 : h * 128 + 128] = field[
                        row : row + 8, g * 128 : g * 128 + 128
                    ]
        return carry

    lax.fori_loop(0, 4, groups, 0)


def tile_sums(slot_ref, field_ref, prev_ref, sums_ref, cells):
    for block in range(8):
        for h in range(8):
            lanes = slice(h * 128, h * 128 + 128)
            state = persist * prev_ref[block, :, lanes] + innovate * field_ref[block, :, lanes]
            rain = jnp.exp(log_mean + log_scale * state)
            cells[h, block : block + 1, :] = jnp.sum(rain, axis=0, keepdims=True)
    dest = lax.broadcasted_iota(jnp.int32, (DEV, 128), 0) * CAP
    lane = lax.broadcasted_iota(jnp.int32, (DEV, 128), 1)
    place = jnp.where(lane < CAP, dest + lane, -1)
    total = jnp.zeros((DEV, 128), F32)
    for h in range(8):
        half = jnp.sum(cells[h], axis=1, keepdims=True)
        for a in range(4):
            tile = (half[2 * a : 2 * a + 1] + half[2 * a + 1 : 2 * a + 2]) * (1.0 / (TILE * TILE))
            total = total + jnp.where(place == slot_ref[a * 8 + h], tile, 0.0)
    sums_ref[...] = total


def next_state(field_ref, prev_ref, state_ref):
    state_ref[...] = persist * prev_ref[...] + innovate * field_ref[...]


def reversal():
    flip = np.zeros((128, 128), np.float32)
    for k in range(1, 128):
        flip[k, 128 - k] = 1.0
    first = np.zeros((128, 128), np.float32)
    first[0, 0] = 1.0
    return np.concatenate([np.eye(128, dtype=np.float32), flip, first], axis=1).astype(ml_dtypes.bfloat16)


def exact_parts(rows):
    a = rows.astype(BF)
    rest = rows - a.astype(F32)
    b = rest.astype(BF)
    return a, b, (rest - b.astype(F32)).astype(BF)


def unfold(ref, group, backward):
    order = range(63, -1, -1) if backward else range(64)
    rows = slice(group * 8, group * 8 + 8)
    return jnp.swapaxes(jnp.stack([ref[rows, k * 128 : k * 128 + 128] for k in order]), 0, 1)


def weight_block(own, rev, flip_ref, d, p):
    rows = [
        jnp.concatenate([a, b, pltpu.roll(b, 1, 0)], axis=1) for a, b in zip(own, rev, strict=True)
    ]
    joint = jnp.concatenate(rows, axis=0)
    dims = ((1,), (1,))
    both = sum(dot(flip_ref[...], part, dims) for part in exact_parts(joint))
    shape = (128, len(own) * 64)
    ka = lax.broadcasted_iota(jnp.int32, shape, 0)
    lane = lax.broadcasted_iota(jnp.int32, shape, 1)
    k0 = ka + 128 * (lane % 64)
    f0 = jnp.where(k0 < N // 2, k0, k0 - N).astype(F32)
    k1 = d * 64 + p(lane // 64)
    f1 = jnp.where(k1 < N // 2, k1, k1 - N).astype(F32)
    width_sq = float((N // 128) * (N // 128))
    envelope = 1.0 + bump_height / (1.0 + (f0 * f0 + f1 * f1) / width_sq)
    return both * (envelope * (0.5 / (N * N)))


def put_weight(out_ref, first, value):
    for b in range(value.shape[1] // 128):
        out_ref[first + b] = value[:, b * 128 : b * 128 + 128]


def far_weights(d_ref, amp_ref, far_ref, flip_ref, out_ref):
    d = d_ref[0]
    own = [row for g in range(FAR // 8 + 1) for row in unfold(amp_ref, g, False)]
    rev = [row for g in range(FAR // 8) for row in unfold(far_ref, g, True)]
    for s in range(0, FAR, 8):
        mirrored = [rev[FAR - 1 - k] for k in range(s, s + 8)]
        value = weight_block(own[s + 1 : s + 9], mirrored, flip_ref, d, lambda k, s=s: k + (s + 1))
        put_weight(out_ref, s // 2, value)


def near_weights(d_ref, amp_ref, near_ref, row_ref, flip_ref, out_ref):
    d = d_ref[0]
    low = d < 64
    middle = d == 64
    own = [row for g in range(5) for row in unfold(amp_ref, g, False)]
    rev = [row for g in range(4 - FAR // 8) for row in unfold(near_ref, g, True)]
    row = row_ref[...]
    turn = lax.broadcasted_iota(jnp.int32, (64, 64), 0) + lax.broadcasted_iota(jnp.int32, (64, 64), 1) == 63
    turned = sum(dot(turn.astype(BF), part) for part in exact_parts(row))
    back = unfold(amp_ref, 0, True)[0]
    own_tail = jnp.where(low, own[32], own[0])
    rev_tail = jnp.where(low, rev[0], jnp.where(middle, back, turned))
    own_all = own[1:32] + [own_tail]
    rev_all = [None] * FAR + [rev[31 - k] for k in range(FAR, 31)] + [rev_tail]

    def plain(k, s):
        return jnp.where(k + s < 31, k + (s + 1), jnp.where(low, 32, 0))

    for s in range(FAR, 32, 8):
        value = weight_block(own_all[s : s + 8], rev_all[s : s + 8], flip_ref, d, lambda k, s=s: plain(k, s))
        put_weight(out_ref, (s - FAR) // 2, value)
    value = weight_block(
        [own[31], jnp.where(middle, row, own_tail)],
        [rev[1], jnp.where(middle, turned, rev_tail)],
        flip_ref,
        d,
        lambda k: jnp.where(k == 0, 31, jnp.where(low, 32, jnp.where(middle, -64 * 64, 0))),
    )
    put_weight(out_ref, 16 - FAR // 2, value)


def catchment_rows(catch_id, owner_map, devices):
    owners = owner_map[:, 0]
    hits = (owners[:, None] == jnp.arange(devices, dtype=jnp.int32)[None, :]).astype(jnp.int32)
    ranks = jnp.sum(hits * (jnp.cumsum(hits, axis=0) - 1), axis=1)
    slot = owners * CAP + ranks
    matches = catch_id.reshape(-1)[:, None] == jnp.arange(owners.shape[0], dtype=jnp.int32)[None, :]
    return jnp.sum(jnp.where(matches, slot[None, :], 0), axis=1)


def shards(white_noise, amplitude, state_prev, catch_id, owner_map, unit_graph, queue_prev):
    d = lax.axis_index(BOTH)
    flat = jax.ShapeDtypeStruct((DEV, 32, 128), F32)
    slab = lax.all_to_all(white_noise.reshape(8, 64, 1024), "col", 0, 0, tiled=True)
    small = np.stack([real_forward(), real_inverse()])
    near = lax.ppermute(amplitude[32 : 64 - FAR], BOTH, [(i, DEV - 1 - i) for i in range(DEV)])
    far = lax.ppermute(amplitude[64 - FAR : 64], "row", [(i, 15 - i) for i in range(16)])
    partner = lax.ppermute(
        amplitude[0:1], BOTH, [(0, 64)] + [(i, DEV - i) for i in range(1, 64)]
    )
    forward_wide, inverse_wide = call(
        widen, [jax.ShapeDtypeStruct((1024, 512), BF)] * 2, flops=100_000_000, bytes_accessed=2_000_000
    )(small)
    tile_slot = catchment_rows(catch_id, owner_map, DEV).astype(jnp.int32)
    device = d.astype(jnp.int32).reshape(1)
    scalar, vector = pl.BlockSpec(memory_space=pltpu.SMEM), pl.BlockSpec(memory_space=pltpu.VMEM)

    def weigh(body, device, blocks, rows, *args):
        return pl.pallas_call(
            body,
            out_shape=jax.ShapeDtypeStruct((blocks, 128, 128), F32),
            grid=(1,),
            in_specs=[scalar, pl.BlockSpec((rows, N), lambda i: (0, 0))] + [vector] * (len(args) - 1),
            compiler_params=pltpu.CompilerParams(vmem_limit_bytes=24 << 20),
            cost_estimate=pl.CostEstimate(flops=300_000_000, bytes_accessed=3_000_000, transcendentals=0),
        )(device, *args)

    flip = reversal()
    near, far = lax.optimization_barrier((near, far))
    near_weight = weigh(near_weights, device, 17 - FAR // 2, 40, amplitude, near, partner.reshape(64, 128), flip)
    far = lax.ppermute(far, "col", [(i, 7 - i) for i in range(8)])
    slab, near_weight, tile_slot, forward_wide, inverse_wide = lax.optimization_barrier(
        (slab, near_weight, tile_slot, forward_wide, inverse_wide)
    )
    tw_row = row_twiddle()
    whole, forward_last, inverse_last = row_tables()
    spec = pl.pallas_call(
        forward_rows,
        out_shape=flat,
        in_specs=[pl.BlockSpec(memory_space=pltpu.MemorySpace.HBM)] * 2 + [vector] * 3,
        scratch_shapes=[
            pltpu.VMEM((33 * 64, 256), F32),
            pltpu.VMEM((8, 64, 1024), F32),
            pltpu.VMEM((1024, 512), BF),
            pltpu.SemaphoreType.DMA((5,)),
        ],
        compiler_params=pltpu.CompilerParams(vmem_limit_bytes=24 << 20),
        cost_estimate=pl.CostEstimate(flops=2_000_000_000, bytes_accessed=6_000_000, transcendentals=0),
    )(slab, forward_wide, tw_row, stacked(whole), stacked(forward_last))
    spec, device = lax.optimization_barrier((spec, device))
    far_weight = weigh(far_weights, device, FAR // 2, FAR + 8, amplitude, far, flip)
    spec, far_weight = lax.optimization_barrier((spec, far_weight))
    spec = lax.all_to_all(spec, BOTH, 0, 0, tiled=True)
    long, short = col_tables(-1.0)
    ilong, ishort = col_tables(1.0)
    tables = np.concatenate([stacked(table) for table in (long, ilong, short, ishort)], axis=0)
    shaped = call(columns, flat)(spec, far_weight, near_weight, col_twiddle(), tables)
    shaped = lax.all_to_all(shaped, BOTH, 0, 0, tiled=True)
    slab_type = jax.ShapeDtypeStruct((8, 64, 1024), F32)
    field = call(inverse_rows, slab_type, [pltpu.VMEM((64 * 64, 128), F32)])(
        shaped, inverse_wide, tw_row, whole, inverse_last
    )
    filtered = lax.all_to_all(field, "col", 0, 0, tiled=True)
    prev = state_prev.reshape(8, 64, 1024)
    sums = pl.pallas_call(
        tile_sums,
        out_shape=jax.ShapeDtypeStruct((DEV, 128), F32),
        in_specs=[scalar] + [vector] * 2,
        scratch_shapes=[pltpu.VMEM((8, 8, 128), F32)],
        compiler_params=pltpu.CompilerParams(vmem_limit_bytes=24 << 20),
        cost_estimate=pl.CostEstimate(flops=5_000_000, bytes_accessed=4_000_000, transcendentals=500_000),
    )(tile_slot, filtered, prev)
    state_new = call(next_state, slab_type, flops=2_000_000)(filtered, prev)
    received = lax.all_to_all(sums.reshape(DEV, 1, 128), BOTH, 0, 0, tiled=True)
    slot_rain = received.sum(axis=(0, 1))[:CAP]
    shifted = jnp.concatenate(
        [queue_prev[1:], jnp.zeros((1, queue_prev.shape[1]), jnp.float32)], axis=0
    )
    flow_queue = shifted + unit_graph * slot_rain[None, :]
    return (state_new.reshape(512, 1024), flow_queue)


def solution(mesh):
    return jax.shard_map(
        shards,
        mesh=mesh,
        in_specs=(
            P("row", "col"),
            P(BOTH, None),
            P("row", "col"),
            P("row", "col"),
            P(),
            P(None, BOTH),
            P(None, BOTH),
        ),
        out_specs=(P("row", "col"), P(None, BOTH)),
        check_vma=False,
    )
```

```python
from functools import partial

import jax
import jax.numpy as jnp
import ml_dtypes
import numpy as np
from jax import lax
from jax.experimental import pallas as pl
from jax.experimental.pallas import tpu as pltpu
from jax.sharding import PartitionSpec as P

TILE = 128
CAP = 32
N = 8192
DEV = 128
FAR = 8
BOTH = ("row", "col")

bump_height = 64.0
persist = 0.8
innovate = 0.6
log_mean = -0.3
log_scale = 0.6

BF = jnp.bfloat16
F32 = jnp.float32


def hi_lo(table):
    table = np.asarray(table, np.float64)
    hi = table.astype(ml_dtypes.bfloat16)
    lo = (table - hi.astype(np.float64)).astype(ml_dtypes.bfloat16)
    return np.concatenate([hi, lo], axis=1)


def stacked(table):
    half = table.shape[1] // 2
    return np.concatenate([table[:, :half], table[:, half:]], axis=0)


def angle(left, right, length):
    return 2.0 * np.pi / length * (np.outer(left, right) % length)


def real_forward():
    turn = angle(np.arange(64), np.arange(64), 64)
    table = np.concatenate([np.cos(turn[:33]), -np.sin(turn[1:32])], axis=0)
    return hi_lo(table)


def real_inverse():
    turn = angle(np.arange(64), np.arange(64), 64)
    real = 2.0 * np.cos(turn[:, :33])
    real[:, 0] = 1.0
    table = np.concatenate([real, -2.0 * np.sin(turn[:, 1:32])], axis=1)
    return hi_lo(table)


def widen(small_ref, fwd_ref, inv_ref):
    tall = (
        lax.broadcasted_iota(jnp.int32, (512, 64), 0) // 8 == lax.broadcasted_iota(jnp.int32, (512, 64), 1)
    ).astype(BF)
    row = lax.broadcasted_iota(jnp.int32, (512, 512), 0)
    col = lax.broadcasted_iota(jnp.int32, (512, 512), 1)
    same = row % 8 == col % 8
    for k, ref in enumerate([fwd_ref, inv_ref]):
        for half in range(2):
            small = small_ref[k, :, half * 64 : half * 64 + 64]
            grown = dot(dot(tall, small).astype(BF), tall, ((1,), (1,)))
            ref[half * 512 : half * 512 + 512, :] = jnp.where(same, grown, 0.0).astype(BF)


def row_twiddle():
    turn = angle(np.arange(33), np.arange(128), N)
    return np.concatenate([np.cos(turn), np.sin(turn)], axis=1).astype(np.float32)


def row_tables():
    turn = angle(np.arange(128), np.arange(128), 128)
    cos, sin = np.cos(turn), np.sin(turn)
    high = (np.arange(128) >= 64).astype(np.float64)[:, None]
    imag = -sin * high
    imag[64] = 1.0
    forward = np.concatenate([cos * high, imag], axis=0)
    top, bottom = 2.0 * cos * high, -2.0 * sin * high
    top[64] = cos[64]
    bottom[64] = 1.0
    inverse = np.concatenate([top, bottom], axis=0)
    return hi_lo(np.block([[cos, sin], [-sin, cos]])), hi_lo(forward), hi_lo(inverse)


def col_tables(sign):
    turn = angle(np.arange(128), np.arange(128), 128)
    cos, sin = np.cos(turn), sign * np.sin(turn)
    long = np.block([[cos, -sin], [sin, cos]])
    turn = angle(np.arange(64), np.arange(64), 64)
    cos, sin = np.kron(np.eye(2), np.cos(turn)), np.kron(np.eye(2), sign * np.sin(turn))
    short = np.block([[cos, sin], [-sin, cos]])
    return hi_lo(long), hi_lo(short)


def col_twiddle():
    turn = angle(np.arange(128), np.arange(128) % 64, N)
    return np.concatenate([np.cos(turn), np.sin(turn)], axis=1).astype(np.float32)


def split(value):
    hi = value.astype(BF)
    return hi, (value - hi.astype(F32)).astype(BF)


def dot(left, right, dims=((1,), (0,))):
    return lax.dot_general(left, right, (dims, ((), ())), preferred_element_type=F32)


def times_table(value, table):
    rows, half = value.shape[0], table.shape[1] // 2
    hi, lo = split(value)
    first = dot(jnp.concatenate([hi, lo], axis=0), table[:, :half])
    return first[:rows] + first[rows:] + dot(hi, table[:, half:])


def table_times(table, value, dims=((1,), (0,))):
    rows = table.shape[0] // 2
    hi, lo = split(value)
    first = dot(table[...], hi, dims)
    return first[:rows] + first[rows:] + dot(table[:rows, :], lo, dims)


def take(ref, group):
    return jnp.swapaxes(ref[:, group * 8 : group * 8 + 8, :], 0, 1)


def put(ref, group, blocks):
    ref[:, group * 8 : group * 8 + 8, :] = jnp.swapaxes(jnp.stack(blocks), 0, 1)


def call(body, out, scratch=(), limit=24, flops=2_000_000_000, bytes_accessed=6_000_000):
    return pl.pallas_call(
        body,
        out_shape=out,
        scratch_shapes=list(scratch),
        compiler_params=pltpu.CompilerParams(vmem_limit_bytes=limit << 20),
        cost_estimate=pl.CostEstimate(flops=flops, bytes_accessed=bytes_accessed, transcendentals=0),
    )


def forward_rows(x_hbm, wide_hbm, tw_ref, whole_ref, last_ref, out_ref, mid, x_ref, wide_ref, sems):
    def fetch(step):
        rows = pl.ds(pl.multiple_of(step * 16, 16), 16)
        return pltpu.make_async_copy(x_hbm.at[:, rows, :], x_ref.at[:, rows, :], sems.at[step])

    table = pltpu.make_async_copy(wide_hbm, wide_ref, sems.at[4])
    table.start()
    for step in range(4):
        fetch(step).start()
    table.wait()

    def groups(step, carry):
        base = pl.multiple_of(step * 16, 16)
        fetch(step).wait()
        left = [x_ref[c, pl.ds(base, 8), h * 128 : h * 128 + 128] for c in range(8) for h in range(8)]
        right = [x_ref[c, pl.ds(base + 8, 8), h * 128 : h * 128 + 128] for c in range(8) for h in range(8)]
        block = jnp.concatenate([jnp.concatenate(left, axis=0), jnp.concatenate(right, axis=0)], axis=1)
        spec = table_times(wide_ref, block)
        for p in range(33):
            cos, sin = tw_ref[p : p + 1, :128], tw_ref[p : p + 1, 128:]
            for g in range(2):
                lanes = slice(g * 128, g * 128 + 128)
                rows = pl.ds(p * 64 + base + g * 8, 8)
                real = spec[p * 8 : p * 8 + 8, lanes]
                if p == 0:
                    mid[rows, :128] = real
                    continue
                if p == 32:
                    mid[rows, :128] = real * cos
                    mid[rows, 128:] = -(real * sin)
                    continue
                imag = spec[(32 + p) * 8 : (32 + p) * 8 + 8, lanes]
                mid[rows, :128] = real * cos + imag * sin
                mid[rows, 128:] = imag * cos - real * sin
        return carry

    lax.fori_loop(0, 4, groups, 0)

    reals, imags = [], []
    for t in range(8):
        rows = mid[(4 * t + 1) * 64 : (4 * t + 5) * 64, :]
        value = table_times(whole_ref, rows, ((1,), (1,)))
        if t == 7:
            rows = jnp.concatenate([jnp.zeros((192, 128), F32), mid[0:64, :128]], axis=0)
            other = table_times(last_ref, rows, ((1,), (1,)))
            q = lax.broadcasted_iota(jnp.int32, (256, 256), 0) % 128
            lane = lax.broadcasted_iota(jnp.int32, (256, 256), 1)
            value = jnp.where((q >= 64) & (lane >= 192), other, value)
        for u in range(2):
            reals.append(value[:128, u * 128 : u * 128 + 128])
            imags.append(value[128:, u * 128 : u * 128 + 128])
        if t % 4 == 3:
            put(out_ref, t // 4, reals)
            put(out_ref, 2 + t // 4, imags)
            reals, imags = [], []


def columns(x_ref, far_ref, near_ref, tw_ref, table_ref, out_ref):
    long_ref, ilong_ref = table_ref.at[0:512, :], table_ref.at[512:1024, :]
    short_ref, ishort_ref = [
        jnp.concatenate([table_ref[k : k + 256, :], table_ref[k + 256 : k + 512, :]], axis=1)
        for k in (1024, 1536)
    ]
    cos, sin = tw_ref[:, :128], tw_ref[:, 128:]

    def some(blocks, extra):
        group = blocks[0] // 8
        real = jnp.concatenate(list(take(x_ref, group)), axis=1)
        imag = jnp.concatenate(list(take(x_ref, 2 + group)), axis=1)
        mid = table_times(long_ref, jnp.concatenate([real, imag], axis=0))
        joints = []
        for u in range(len(blocks)):
            real, imag = mid[:128, u * 128 : u * 128 + 128], mid[128:, u * 128 : u * 128 + 128]
            joints.append(jnp.concatenate([real * cos + imag * sin, imag * cos - real * sin], axis=1))
        spec = times_table(jnp.concatenate(joints, axis=0), short_ref)
        joints = []
        for u, b in enumerate(blocks):
            weight = far_ref[b] if b < FAR // 2 else near_ref[b - FAR // 2]
            joints.append(spec[u * 128 : u * 128 + 128] * jnp.concatenate([weight, weight], axis=1))
        if extra:
            weight = near_ref[16 - FAR // 2]
            u = len(blocks) - 1
            joints.append(spec[u * 128 : u * 128 + 128] * jnp.concatenate([weight, weight], axis=1))
        mixed = times_table(jnp.concatenate(joints, axis=0), ishort_ref)
        reals, imags = [], []
        for u in range(len(joints)):
            real, imag = mixed[u * 128 : u * 128 + 128, :128], mixed[u * 128 : u * 128 + 128, 128:]
            reals.append(real * cos - imag * sin)
            imags.append(imag * cos + real * sin)
        done = table_times(
            ilong_ref,
            jnp.concatenate([jnp.concatenate(reals, axis=1), jnp.concatenate(imags, axis=1)], axis=0),
        )
        last = len(joints) - 1
        put(out_ref, group, [done[:128, u * 128 : u * 128 + 128] for u in range(8)])
        put(out_ref, 2 + group, [done[128:, u * 128 : u * 128 + 128] for u in [*range(7), last]])

    some(range(8), False)
    some(range(8, 16), True)


def inverse_rows(x_ref, wide_ref, tw_ref, whole_ref, last_ref, out_ref, mid):

    def place(p, value):
        cos, sin = tw_ref[p : p + 1, :128], tw_ref[p : p + 1, 128:]
        real, imag = value[:, :128], value[:, 128:]
        mid[p * 64 : p * 64 + 64, :] = real * cos - imag * sin
        if p < 32:
            mid[(32 + p) * 64 : (33 + p) * 64, :] = imag * cos + real * sin

    for t in range(8):
        if t % 4 == 0:
            reals, imags = take(x_ref, t // 4), take(x_ref, 2 + t // 4)
        u = t % 4 * 2
        real = jnp.concatenate([reals[u], reals[u + 1]], axis=1)
        imag = jnp.concatenate([imags[u], imags[u + 1]], axis=1)
        joint = jnp.concatenate([real, imag], axis=0).T
        if t == 7:
            slot = lax.broadcasted_iota(jnp.int32, (256, 256), 0)
            q = lax.broadcasted_iota(jnp.int32, (256, 256), 1) % 128
            mid[0:64, :] = times_table(joint[192:, :], last_ref)
            joint = jnp.where((slot >= 192) & (q >= 64), 0.0, joint)
        result = times_table(joint, whole_ref)
        for k in range(4):
            place(4 * t + k + 1, result[k * 64 : k * 64 + 64, :])

    def groups(step, carry):
        base = pl.multiple_of(step * 16, 16)
        left = [mid[pl.ds(pp * 64 + base, 8), :] for pp in range(64)]
        right = [mid[pl.ds(pp * 64 + base + 8, 8), :] for pp in range(64)]
        block = jnp.concatenate([jnp.concatenate(left, axis=0), jnp.concatenate(right, axis=0)], axis=1)
        field = table_times(wide_ref, block)
        for c in range(8):
            for h in range(8):
                row = (c * 8 + h) * 8
                for g in range(2):
                    out_ref[c, pl.ds(base + g * 8, 8), h * 128 : h * 128 + 128] = field[
                        row : row + 8, g * 128 : g * 128 + 128
                    ]
        return carry

    lax.fori_loop(0, 4, groups, 0)


def tile_sums(slot_ref, field_ref, prev_ref, sums_ref, cells):
    for block in range(8):
        for h in range(8):
            lanes = slice(h * 128, h * 128 + 128)
            state = persist * prev_ref[block, :, lanes] + innovate * field_ref[block, :, lanes]
            rain = jnp.exp(log_mean + log_scale * state)
            cells[h, block : block + 1, :] = jnp.sum(rain, axis=0, keepdims=True)
    dest = lax.broadcasted_iota(jnp.int32, (DEV, 128), 0) * CAP
    lane = lax.broadcasted_iota(jnp.int32, (DEV, 128), 1)
    place = jnp.where(lane < CAP, dest + lane, -1)
    total = jnp.zeros((DEV, 128), F32)
    for h in range(8):
        half = jnp.sum(cells[h], axis=1, keepdims=True)
        for a in range(4):
            tile = (half[2 * a : 2 * a + 1] + half[2 * a + 1 : 2 * a + 2]) * (1.0 / (TILE * TILE))
            total = total + jnp.where(place == slot_ref[a * 8 + h], tile, 0.0)
    sums_ref[...] = total


def next_state(field_ref, prev_ref, state_ref):
    state_ref[...] = persist * prev_ref[...] + innovate * field_ref[...]


def reversal():
    flip = np.zeros((128, 128), np.float32)
    for k in range(1, 128):
        flip[k, 128 - k] = 1.0
    first = np.zeros((128, 128), np.float32)
    first[0, 0] = 1.0
    return np.concatenate([np.eye(128, dtype=np.float32), flip, first], axis=1).astype(ml_dtypes.bfloat16)


def exact_parts(rows):
    a = rows.astype(BF)
    rest = rows - a.astype(F32)
    b = rest.astype(BF)
    return a, b, (rest - b.astype(F32)).astype(BF)


def unfold(ref, group, backward):
    order = range(63, -1, -1) if backward else range(64)
    rows = slice(group * 8, group * 8 + 8)
    return jnp.swapaxes(jnp.stack([ref[rows, k * 128 : k * 128 + 128] for k in order]), 0, 1)


def weight_block(own, rev, flip_ref, d, p):
    rows = [
        jnp.concatenate([a, b, pltpu.roll(b, 1, 0)], axis=1) for a, b in zip(own, rev, strict=True)
    ]
    joint = jnp.concatenate(rows, axis=0)
    dims = ((1,), (1,))
    both = sum(dot(flip_ref[...], part, dims) for part in exact_parts(joint))
    shape = (128, len(own) * 64)
    ka = lax.broadcasted_iota(jnp.int32, shape, 0)
    lane = lax.broadcasted_iota(jnp.int32, shape, 1)
    k0 = ka + 128 * (lane % 64)
    f0 = jnp.where(k0 < N // 2, k0, k0 - N).astype(F32)
    k1 = d * 64 + p(lane // 64)
    f1 = jnp.where(k1 < N // 2, k1, k1 - N).astype(F32)
    width_sq = float((N // 128) * (N // 128))
    envelope = 1.0 + bump_height / (1.0 + (f0 * f0 + f1 * f1) / width_sq)
    return both * (envelope * (0.5 / (N * N)))


def put_weight(out_ref, first, value):
    for b in range(value.shape[1] // 128):
        out_ref[first + b] = value[:, b * 128 : b * 128 + 128]


def far_weights(d_ref, amp_ref, far_ref, flip_ref, out_ref):
    d = d_ref[0]
    own = [row for g in range(FAR // 8 + 1) for row in unfold(amp_ref, g, False)]
    rev = [row for g in range(FAR // 8) for row in unfold(far_ref, g, True)]
    for s in range(0, FAR, 8):
        mirrored = [rev[FAR - 1 - k] for k in range(s, s + 8)]
        value = weight_block(own[s + 1 : s + 9], mirrored, flip_ref, d, lambda k, s=s: k + (s + 1))
        put_weight(out_ref, s // 2, value)


def near_weights(d_ref, amp_ref, near_ref, row_ref, flip_ref, out_ref):
    d = d_ref[0]
    low = d < 64
    middle = d == 64
    own = [row for g in range(5) for row in unfold(amp_ref, g, False)]
    rev = [row for g in range(4 - FAR // 8) for row in unfold(near_ref, g, True)]
    row = row_ref[...]
    turn = lax.broadcasted_iota(jnp.int32, (64, 64), 0) + lax.broadcasted_iota(jnp.int32, (64, 64), 1) == 63
    turned = sum(dot(turn.astype(BF), part) for part in exact_parts(row))
    back = unfold(amp_ref, 0, True)[0]
    own_tail = jnp.where(low, own[32], own[0])
    rev_tail = jnp.where(low, rev[0], jnp.where(middle, back, turned))
    own_all = own[1:32] + [own_tail]
    rev_all = [None] * FAR + [rev[31 - k] for k in range(FAR, 31)] + [rev_tail]

    def plain(k, s):
        return jnp.where(k + s < 31, k + (s + 1), jnp.where(low, 32, 0))

    for s in range(FAR, 32, 8):
        value = weight_block(own_all[s : s + 8], rev_all[s : s + 8], flip_ref, d, lambda k, s=s: plain(k, s))
        put_weight(out_ref, (s - FAR) // 2, value)
    value = weight_block(
        [own[31], jnp.where(middle, row, own_tail)],
        [rev[1], jnp.where(middle, turned, rev_tail)],
        flip_ref,
        d,
        lambda k: jnp.where(k == 0, 31, jnp.where(low, 32, jnp.where(middle, -64 * 64, 0))),
    )
    put_weight(out_ref, 16 - FAR // 2, value)


def catchment_rows(catch_id, owner_map, devices):
    owners = owner_map[:, 0]
    hits = (owners[:, None] == jnp.arange(devices, dtype=jnp.int32)[None, :]).astype(jnp.int32)
    ranks = jnp.sum(hits * (jnp.cumsum(hits, axis=0) - 1), axis=1)
    slot = owners * CAP + ranks
    matches = catch_id.reshape(-1)[:, None] == jnp.arange(owners.shape[0], dtype=jnp.int32)[None, :]
    return jnp.sum(jnp.where(matches, slot[None, :], 0), axis=1)


def shards(white_noise, amplitude, state_prev, catch_id, owner_map, unit_graph, queue_prev):
    d = lax.axis_index(BOTH)
    flat = jax.ShapeDtypeStruct((DEV, 32, 128), F32)
    slab = lax.all_to_all(white_noise.reshape(8, 64, 1024), "col", 0, 0, tiled=True)
    small = np.stack([real_forward(), real_inverse()])
    near = lax.ppermute(amplitude[32 : 64 - FAR], BOTH, [(i, DEV - 1 - i) for i in range(DEV)])
    far = lax.ppermute(amplitude[64 - FAR : 64], "row", [(i, 15 - i) for i in range(16)])
    partner = lax.ppermute(
        amplitude[0:1], BOTH, [(0, 64)] + [(i, DEV - i) for i in range(1, 64)]
    )
    forward_wide, inverse_wide = call(
        widen, [jax.ShapeDtypeStruct((1024, 512), BF)] * 2, flops=100_000_000, bytes_accessed=2_000_000
    )(small)
    tile_slot = catchment_rows(catch_id, owner_map, DEV).astype(jnp.int32)
    device = d.astype(jnp.int32).reshape(1)
    scalar, vector = pl.BlockSpec(memory_space=pltpu.SMEM), pl.BlockSpec(memory_space=pltpu.VMEM)

    def weigh(body, device, blocks, rows, *args):
        return pl.pallas_call(
            body,
            out_shape=jax.ShapeDtypeStruct((blocks, 128, 128), F32),
            grid=(1,),
            in_specs=[scalar, pl.BlockSpec((rows, N), lambda i: (0, 0))] + [vector] * (len(args) - 1),
            compiler_params=pltpu.CompilerParams(vmem_limit_bytes=24 << 20),
            cost_estimate=pl.CostEstimate(flops=300_000_000, bytes_accessed=3_000_000, transcendentals=0),
        )(device, *args)

    flip = reversal()
    near, far = lax.optimization_barrier((near, far))
    near_weight = weigh(near_weights, device, 17 - FAR // 2, 40, amplitude, near, partner.reshape(64, 128), flip)
    far = lax.ppermute(far, "col", [(i, 7 - i) for i in range(8)])
    slab, near_weight, tile_slot, forward_wide, inverse_wide = lax.optimization_barrier(
        (slab, near_weight, tile_slot, forward_wide, inverse_wide)
    )
    tw_row = row_twiddle()
    whole, forward_last, inverse_last = row_tables()
    spec = pl.pallas_call(
        forward_rows,
        out_shape=flat,
        in_specs=[pl.BlockSpec(memory_space=pltpu.MemorySpace.HBM)] * 2 + [vector] * 3,
        scratch_shapes=[
            pltpu.VMEM((33 * 64, 256), F32),
            pltpu.VMEM((8, 64, 1024), F32),
            pltpu.VMEM((1024, 512), BF),
            pltpu.SemaphoreType.DMA((5,)),
        ],
        compiler_params=pltpu.CompilerParams(vmem_limit_bytes=24 << 20),
        cost_estimate=pl.CostEstimate(flops=2_000_000_000, bytes_accessed=6_000_000, transcendentals=0),
    )(slab, forward_wide, tw_row, stacked(whole), stacked(forward_last))
    spec, device = lax.optimization_barrier((spec, device))
    far_weight = weigh(far_weights, device, FAR // 2, FAR + 8, amplitude, far, flip)
    spec, far_weight = lax.optimization_barrier((spec, far_weight))
    spec = lax.all_to_all(spec, BOTH, 0, 0, tiled=True)
    long, short = col_tables(-1.0)
    ilong, ishort = col_tables(1.0)
    tables = np.concatenate([stacked(table) for table in (long, ilong, short, ishort)], axis=0)
    shaped = call(columns, flat)(spec, far_weight, near_weight, col_twiddle(), tables)
    shaped = lax.all_to_all(shaped, BOTH, 0, 0, tiled=True)
    slab_type = jax.ShapeDtypeStruct((8, 64, 1024), F32)
    field = call(inverse_rows, slab_type, [pltpu.VMEM((64 * 64, 128), F32)])(
        shaped, inverse_wide, tw_row, whole, inverse_last
    )
    filtered = lax.all_to_all(field, "col", 0, 0, tiled=True)
    prev = state_prev.reshape(8, 64, 1024)
    sums = pl.pallas_call(
        tile_sums,
        out_shape=jax.ShapeDtypeStruct((DEV, 128), F32),
        in_specs=[scalar] + [vector] * 2,
        scratch_shapes=[pltpu.VMEM((8, 8, 128), F32)],
        compiler_params=pltpu.CompilerParams(vmem_limit_bytes=24 << 20),
        cost_estimate=pl.CostEstimate(flops=5_000_000, bytes_accessed=4_000_000, transcendentals=500_000),
    )(tile_slot, filtered, prev)
    state_new = call(next_state, slab_type, flops=2_000_000)(filtered, prev)
    received = lax.all_to_all(sums.reshape(DEV, 1, 128), BOTH, 0, 0, tiled=True)
    slot_rain = received.sum(axis=(0, 1))[:CAP]
    shifted = jnp.concatenate(
        [queue_prev[1:], jnp.zeros((1, queue_prev.shape[1]), jnp.float32)], axis=0
    )
    flow_queue = shifted + unit_graph * slot_rain[None, :]
    return (state_new.reshape(512, 1024), flow_queue)


def solution(mesh):
    return jax.shard_map(
        shards,
        mesh=mesh,
        in_specs=(
            P("row", "col"),
            P(BOTH, None),
            P("row", "col"),
            P("row", "col"),
            P(),
            P(None, BOTH),
            P(None, BOTH),
        ),
        out_specs=(P("row", "col"), P(None, BOTH)),
        check_vma=False,
    )
```
